32 devices in a mesh: prow: 8 (over y, x, core), pcol: 4 (over z).
Axes of the slice: x: 2, y: 2, z: 4, core: 2. Of those that a mesh axis runs over, the one named last changes fastest.
Arguments:
- panel: float32 [16, 1024, 128], P('pcol', 'prow'), may hold values from -8 to 192, as said below
- strip: float32 [16, 1024, 2, 512], P(None, 'prow', None, 'pcol'), may hold values from -6 to 6
- factor: float32 [16, 1024, 2, 512], P(None, 'prow', None, 'pcol'), may hold values from -0.125 to 0.125
- inv_diag: float32 [8, 128, 128], replicated, may hold values from -0.24 to 1.4, as said below
- rhs: float32 [16, 1024, 256], P(None, 'prow'), may hold values from -6 to 6
Outputs:
- panel_factor: float32 [16, 1024, 128], P('pcol', 'prow')
- new_strip: float32 [16, 1024, 2, 512], P(None, 'prow', None, 'pcol')
- forward: float32 [16, 1024, 256], P(None, 'prow')
The draws below stay inside these ranges and needn't reach their ends.
Inputs may be any that keep to these rules, and one draw needn't show every extreme that they name: Row tile 8 of the panel, read as in the first step, is symmetric positive definite. `inv_diag`: every block is lower triangular with a positive diagonal.
All inputs are finite; a program needn't handle non-finite values.
Results may differ from the reference program's by a relative error of at most 0.00018.
Values sent between devices are 32-bit elements; how exact they have to be, the bound alone decides.
A program may use at most 64 MiB of HBM per device.

```python
import jax
import jax.numpy as jnp
from jax import lax

TILE = 128
TPD = 16
KF = 2
CTD = 2
NRHS = 256
NROWS = 16384
KSWEEP = 8
KSTRIP = 8
N_PROW = 8
N_PCOL = 4


def draw_panel(key, part):
    key_base, key_points, key_nugget = jax.random.split(key, 3)
    base = jax.random.truncated_normal(key_base, -4.0, 4.0, (NROWS, TILE), jnp.float32) * 2.0
    points = jax.random.uniform(key_points, (TILE, 1, 3), jnp.float32, 0.0, 1.0)
    distance = jnp.sum(jnp.abs(points - jnp.transpose(points, (1, 0, 2))), axis=2)
    kernel = jnp.exp(-distance / 0.5)
    nugget = jax.random.uniform(key_nugget, (TILE,), jnp.float32, 0.5, 2.0)
    unit = jnp.eye(TILE, dtype=jnp.float32)
    block = 64.0 * (kernel + unit * nugget[None, :])
    whole = lax.dynamic_update_slice(base, block, (KSWEEP * TILE, 0))
    return whole.reshape(TPD, NROWS // TPD, TILE)


def draw_inv_diag(key, part):
    key_off, key_diag = jax.random.split(key, 2)
    off_part = jax.random.truncated_normal(key_off, -3.0, 3.0, (KSWEEP, TILE, TILE), jnp.float32) * 0.08
    diag_values = jax.random.uniform(key_diag, (KSWEEP, TILE, 1), jnp.float32, 0.6, 1.4)
    strict_lower = jnp.tril(jnp.ones((TILE, TILE), jnp.float32), -1)
    unit = jnp.eye(TILE, dtype=jnp.float32)
    return off_part * strict_lower[None] + unit[None] * diag_values


def levels(key, dims, shards, low, largest):
    gain = 1.0
    for position, parts in shards:
        steps = jax.random.uniform(jax.random.fold_in(jax.random.fold_in(key, 6), position), (parts,), jnp.float32, low / len(shards), largest / len(shards))
        gain = gain * jnp.repeat(jnp.exp(steps), dims[position] // parts).reshape((-1,) + (1,) * (len(dims) - 1 - position))
    return gain


def bell_draw(own_key, shape, width, most, cuts=(), kind=jnp.bfloat16):
    result = width * jax.random.normal(own_key, shape, jnp.float32)
    if cuts:
        result = result * levels(own_key, shape, cuts, -0.22, 0.18)
    return jnp.clip(result, -most, most).astype(kind)


def setup_inputs(seed: int = 0) -> dict:
    splits = jax.random.split(jax.random.key(seed), 6)
    return {
        "panel": draw_panel(jax.random.fold_in(splits[5], 71), 0),
        "strip": bell_draw(splits[1], (TPD, N_PROW * TILE, CTD, N_PCOL * TILE), 1.0, 6.0, ((1, 8), (3, 4)), jnp.float32),
        "factor": bell_draw(splits[2], (TPD, N_PROW * TILE, KF, N_PCOL * TILE), (16 * TILE) ** -0.5, 0.125, ((1, 8), (3, 4)), jnp.float32),
        "inv_diag": draw_inv_diag(jax.random.fold_in(splits[5], 71), 0),
        "rhs": bell_draw(splits[4], (TPD, N_PROW * TILE, NRHS), 1.0, 6.0, ((1, 8),), jnp.float32),
    }


def reference(panel, strip, factor, inv_diag, rhs):
    highest = lax.Precision.HIGHEST
    panel_mat = panel.reshape(NROWS, TILE)
    strip_mat = strip.reshape(NROWS, KSTRIP * TILE)
    factor_mat = factor.reshape(NROWS, KSWEEP * TILE)
    rhs_mat = rhs.reshape(NROWS, NRHS)
    diag_block = panel_mat[KSWEEP * TILE:(KSWEEP + 1) * TILE]
    diag_factor = jnp.linalg.cholesky(diag_block)
    inverse = jax.scipy.linalg.solve_triangular(diag_factor, jnp.eye(TILE, dtype=diag_block.dtype), lower=True)
    scaled = jnp.dot(panel_mat, inverse.T, precision=highest)
    tile_index = jnp.arange(NROWS) // TILE
    below_part = jnp.where((tile_index > KSWEEP)[:, None], scaled, 0.0)
    panel_out = below_part.at[KSWEEP * TILE:(KSWEEP + 1) * TILE].set(diag_factor)
    column = below_part[(KSWEEP + 1) * TILE:(KSWEEP + 1 + KSTRIP) * TILE]
    strip_out = strip_mat - jnp.dot(below_part, column.T, precision=highest)
    solved = []
    for sweep_step in range(KSWEEP):
        residue = rhs_mat[sweep_step * TILE:(sweep_step + 1) * TILE]
        if sweep_step > 0:
            earlier = jnp.concatenate(solved, axis=0)
            block_row = factor_mat[sweep_step * TILE:(sweep_step + 1) * TILE, :sweep_step * TILE]
            residue = residue - jnp.dot(block_row, earlier, precision=highest)
        solved.append(jnp.dot(inv_diag[sweep_step], residue, precision=highest))
    stacked = jnp.concatenate(solved, axis=0)
    remains = rhs_mat - jnp.dot(factor_mat, stacked, precision=highest)
    panel_solution = jnp.dot(inverse, remains[KSWEEP * TILE:(KSWEEP + 1) * TILE], precision=highest)
    remains = remains - jnp.dot(below_part, panel_solution, precision=highest)
    remains = remains.at[:KSWEEP * TILE].set(stacked)
    remains = remains.at[KSWEEP * TILE:(KSWEEP + 1) * TILE].set(panel_solution)
    return (panel_out.reshape(panel.shape), strip_out.reshape(strip.shape), remains.reshape(rhs.shape))
```

```python
import functools

import jax
import jax.numpy as jnp
from jax import lax
from jax.experimental import pallas as pl
from jax.experimental.pallas import tpu as pltpu
from jax.sharding import PartitionSpec as P

HIGHEST = lax.Precision.HIGHEST
HIGH = lax.Precision.HIGH
MESH = pl.DeviceIdType.MESH
SPLIT = 2
SKEW = 2


def dot(a, b, precision=HIGHEST):
    return jnp.dot(a, b, precision=precision, preferred_element_type=jnp.float32)


def when(cond, body):
    if cond is True:
        body()
    elif cond is not False:
        pl.when(cond)(body)


def flip(v, m):
    return v + m - 2 * m * lax.rem(lax.div(v, m), 2)


def kernel(
    R, C, CTD, KF,
    panel, strip, factor, inv_diag, rhs,
    panel_out, strip_out, forward,
    pan_all, diag, col, colt, ftop, ftri, brow, y, fbuf, rbuf, sbuf, dbuf, own, rin, lin, pbuf, tri, inv, inv_t, ps,
    z_send, z_recv, p_send, p_recv, r_send, r_recv, l_send, l_recv, in_sem, f_out, s_out, p_out,
):
    r = lax.axis_index("prow")
    c = lax.axis_index("pcol")
    A, TILE, _ = panel.shape
    I = factor.shape[0]
    KS = KF * C
    full = KS == R
    i0 = KS // R
    H = TILE // SPLIT
    N = (I - i0) * SPLIT

    def target(row):
        return jnp.where(row == 0, KS, row) if full else row

    def slot(row):
        return target(row) if full else jnp.minimum(row, KS)

    def tiles_of(row):
        return target(row) if full else jnp.where(row <= KS, row, 0)

    first = jnp.where(r == 0, KS // R, 0) if full else 0
    b_own = True if full else r < KS
    k_own = r == KS % R

    def load(n, src, dst):
        return pltpu.make_async_copy(src, dst, in_sem.at[n])

    loads = [
        load(0, panel, pan_all.at[pl.ds(c * A, A)]),
        load(1, factor.at[first], ftop),
        load(2, rhs.at[0], brow.at[jnp.minimum(r, KS - 1)]),
        load(3, rhs.at[KS // R], brow.at[KS]),
        load(4, inv_diag, dbuf),
        load(5, factor, fbuf),
        load(6, rhs, rbuf),
        load(7, strip, sbuf),
    ]
    conds = [True, True, b_own, k_own, True, True, True, True]
    for cond, one in zip(conds, loads):
        when(cond, one.start)

    dims = []
    m = 2
    while m < R:
        dims.append(m)
        m *= 2
    seqs = (dims + [1], dims[::-1] + [1])

    barrier = pltpu.get_barrier_semaphore()

    @pl.loop(1, C)
    def _(d):
        pl.semaphore_signal(barrier, inc=1, device_id={"pcol": lax.rem(c + d, C)}, device_id_type=MESH)

    for m in dims + [1]:
        pl.semaphore_signal(barrier, inc=1, device_id={"prow": flip(r, m)}, device_id_type=MESH)
    pl.semaphore_wait(barrier, C - 1 + len(dims) + 1)

    PAN, DIA = KF, KF + 1
    dia_plane = KS // R // A

    def z_copy(kind, d, source, place):
        if kind < KF:
            src = dst = ftri.at[slot(r), kind * C + source]
        elif kind == PAN:
            src = dst = pan_all.at[pl.ds(source * A, A)]
        else:
            src, dst = pan_all.at[KS // R], diag
        return pltpu.make_async_remote_copy(
            src_ref=src, dst_ref=dst, send_sem=z_send.at[kind, d - 1], recv_sem=z_recv.at[kind, d - 1],
            device_id={"pcol": place}, device_id_type=MESH,
        )

    def z_cond(kind, source):
        if kind == DIA:
            return jnp.logical_and(k_own, source == dia_plane)
        return kind * C + source < tiles_of(r) if kind < KF else True

    def z_start(kind):
        for d in range(1, C):
            when(z_cond(kind, c), lambda d=d: z_copy(kind, d, c, lax.rem(c + d, C)).start())

    def z_wait_send(kind):
        for d in range(1, C):
            when(z_cond(kind, c), lambda d=d: z_copy(kind, d, c, lax.rem(c + d, C)).wait_send())

    def z_wait_recv(kind, only=None):
        for d in range(1, C) if only is None else (only,):
            source = lax.rem(c + C - d, C)
            when(z_cond(kind, source), lambda d=d, source=source: z_copy(kind, d, source, c).wait_recv())

    B0, BK, DG, CL = 0, SPLIT, 2 * SPLIT, 2 * SPLIT + 1
    TL = CL + CTD

    def wanted(s):
        return KS + 1 + s * C + c

    def place(kind, row):
        if kind < BK:
            return brow.at[jnp.minimum(row, KS - 1), pl.ds((kind - B0) * H, H)]
        if kind < DG:
            return brow.at[KS, pl.ds((kind - BK) * H, H)]
        if kind == DG:
            return diag
        return col.at[kind - CL]

    def p_cond(kind, row):
        if kind < BK:
            return True if full else row < KS
        if kind <= DG:
            return row == KS % R
        return row == lax.rem(wanted(kind - CL), R)

    def node(d):
        t = r
        for m in seqs[0]:
            if d & m:
                t = flip(t, m)
        return t

    def p_copy(item, ref, row, d, m):
        bit = m.bit_length() - 1
        return pltpu.make_async_remote_copy(
            src_ref=ref, dst_ref=ref, send_sem=p_send.at[item, d // 2, bit], recv_sem=p_recv.at[item, row],
            device_id={"prow": flip(r, m)}, device_id_type=MESH,
        )

    def tile(n, order):
        d = 2 * lax.rem(n, C // 2) + order
        return lax.div(n, C // 2) * C + lax.rem(c + C - d, C)

    def each(kinds, row, act):
        for kind in kinds:
            if kind == "tiles":
                for order in range(2):
                    def one(n, carry, order=order):
                        j = tile(n, order)

                        @pl.when(j < tiles_of(row))
                        def _():
                            act(TL + j, ftri.at[slot(row), j], row, order)

                        return carry

                    lax.fori_loop(0, KF * C // 2, one, 0)
            else:
                when(p_cond(kind, row), lambda kind=kind: act(kind, place(kind, row), row, kind % 2))

    def outs(d, order):
        seq = seqs[order]
        at = max([n for n, m in enumerate(seq) if d & m], default=-1)
        return seq[at + 1:]

    def spread(d, kinds):
        def act(item, ref, row, order):
            if d:
                p_copy(item, ref, row, d, 1).wait_recv()
            for m in outs(d, order):
                p_copy(item, ref, row, d, m).start()

        each(kinds, node(d), act)

    def drain(kinds):
        for d in range(0, R, 2):
            def act(item, ref, row, order, d=d):
                for m in outs(d, order):
                    p_copy(item, ref, row, d, m).wait_send()

            each(kinds, node(d), act)

    def odd(row, kinds):
        @pl.when(lax.rem(r + row, 2) == 1)
        def _():
            each(kinds, row, lambda item, ref, row, order: p_copy(item, ref, row, 0, 1).wait_recv())

    near = [d for d in range(2, R, 2) if d & (d - 1) == 0]
    far = [d for d in range(2, R, 2) if d & (d - 1) != 0]
    bs = tuple(range(B0, BK))
    bk = tuple(range(BK, DG))
    cols = tuple(range(CL, TL))

    loads[0].wait()
    z_start(DIA)

    @pl.when(z_cond(DIA, c))
    def _():
        diag[...] = pan_all[KS // R]

    loads[1].wait()
    for s in range(KF):
        @pl.when(z_cond(s, c))
        def _(s=s):
            ftri[slot(r), s * C + c] = ftop[pl.ds(s, TILE, stride=KF), :]

    for kind in range(KF):
        z_start(kind)
    when(b_own, loads[2].wait)
    when(k_own, loads[3].wait)
    z_wait_recv(DIA)
    spread(0, (DG,))
    spread(0, bs + bk)
    for kind in range(KF):
        z_wait_recv(kind)
    spread(0, ("tiles",))
    z_start(PAN)
    for d in near + far:
        spread(d, (DG,))
    odd(KS % R, (DG,))

    lanes = lax.broadcasted_iota(jnp.int32, (TILE, TILE), 1)
    rows = lax.broadcasted_iota(jnp.int32, (TILE, TILE), 0)
    tri[...] = diag[...]
    inv[...] = jnp.where(lanes == rows, 1.0, 0.0)

    def eliminate(k, carry):
        lane = lanes[0:1]
        row = tri[pl.ds(k, 1), :]
        whole = tri[...]
        pivot = jnp.sum(jnp.where(lane == k, row, 0.0), axis=1, keepdims=True)
        scale = 1.0 / jnp.sqrt(pivot)
        lrow = jnp.where(lane >= k, row * scale, 0.0)
        column = jnp.sum(jnp.where(lanes == k, whole, 0.0), axis=1, keepdims=True)
        lcol = jnp.where(rows[:, 0:1] > k, column * scale, 0.0)
        wrow = inv[pl.ds(k, 1), :] * scale
        tri[...] = whole - lcol * lrow
        inv[...] = inv[...] - lcol * wrow
        tri[pl.ds(k, 1), :] = lrow
        inv[pl.ds(k, 1), :] = wrow
        return carry

    def part(n, of):
        lax.fori_loop(n * TILE // of, (n + 1) * TILE // of, eliminate, 0)

    part(0, 4)
    for d in near:
        spread(d, bs + bk)
    part(1, 4)
    for d in near:
        spread(d, ("tiles",))
    part(2, 4)
    for d in far:
        spread(d, bs + bk + ("tiles",))
    part(3, 4)
    inv_t[...] = inv[...].T

    loads[4].wait()

    def advance(t, carry):
        odd(t, bs)

        @pl.when(t > 0)
        def _():
            odd(lax.rem(t, R), ("tiles",))

        def reach(j, total):
            return total - dot(ftri[t, j], y[j])

        y[t] = dot(dbuf[t], lax.fori_loop(0, t, reach, brow[t]))
        return carry

    lax.fori_loop(0, KS, advance, 0)
    odd(KS % R, bk + ("tiles",))
    ps[...] = dot(
        inv[...], lax.fori_loop(0, KS, lambda j, total: total - dot(ftri[KS, j], y[j]), brow[KS])
    )

    def up_copy(n, src):
        return pltpu.make_async_remote_copy(
            src_ref=src.at[n], dst_ref=rin.at[n], send_sem=r_send.at[n], recv_sem=r_recv.at[n],
            device_id={"pcol": jnp.minimum(c + 1, C - 1)}, device_id_type=MESH,
        )

    def down_copy(n, src):
        return pltpu.make_async_remote_copy(
            src_ref=src.at[n], dst_ref=lin.at[n], send_sem=l_send.at[n], recv_sem=l_recv.at[n],
            device_id={"pcol": jnp.maximum(c - 1, 0)}, device_id_type=MESH,
        )

    loads[5].wait()

    def product(i, carry):
        total = dot(fbuf[i, pl.ds(0, TILE, stride=KF), :], y[c], HIGH)
        for s in range(1, KF):
            total = total + dot(fbuf[i, pl.ds(s, TILE, stride=KF), :], y[s * C + c], HIGH)
        for h in range(SPLIT):
            n = (i - i0) * SPLIT + h
            own[n] = total[h * H:(h + 1) * H]

            @pl.when(c == 0)
            def _():
                up_copy(n, own).start()

            @pl.when(c == C - 1)
            def _():
                down_copy(n, own).start()

        return carry

    lax.fori_loop(i0, I, product, 0)

    z_wait_recv(PAN)
    for s in range(CTD):
        @pl.when(p_cond(CL + s, r))
        def _(s=s):
            col[s] = pan_all[wanted(s) // R]

    spread(0, cols)
    for a in range(A):
        tile_a = (c * A + a) * R + r
        pbuf[a] = jnp.where(tile_a > KS, dot(pan_all[c * A + a], inv_t[...]), 0.0)

        @pl.when(tile_a == KS)
        def _(a=a):
            pbuf[a] = tri[...].T

    pout = pltpu.make_async_copy(pbuf, panel_out, p_out)
    pout.start()
    for d in near + far:
        spread(d, cols)
    for s in range(CTD):
        odd(lax.rem(wanted(s), R), (CL + s,))
    for s in range(CTD):
        colt[s] = dot(col[s], inv_t[...]).T

    loads[6].wait()
    loads[7].wait()

    def f_copy(i):
        return pltpu.make_async_copy(rbuf.at[i], forward.at[i], f_out.at[i])

    def strip_copy(i):
        return pltpu.make_async_copy(sbuf.at[i], strip_out.at[i], s_out.at[i])

    for i in range(i0):
        rbuf[i] = y[i * R + r]
        f_copy(i).start()
        strip_copy(i).start()

    def strip_row(i):
        below = jnp.where(i * R + r > KS, dot(pan_all[i], inv_t[...], HIGH), 0.0)
        for s in range(CTD):
            at = pl.ds(s, TILE, stride=CTD)
            sbuf[i, at, :] = sbuf[i, at, :] - dot(below, colt[s], HIGH)
        strip_copy(i).start()
        rbuf[i] = rbuf[i] - dot(below, ps[...], HIGH)

    def step(m, carry):
        nr = m - c * SKEW
        nl = m - (C - 1 - c) * SKEW
        nf = m - jnp.maximum(c, C - 1 - c) * SKEW

        @pl.when(jnp.logical_and(c > 0, jnp.logical_and(nr >= 0, nr < N)))
        def _():
            up_copy(nr, rin).wait_recv()
            rin[nr] = rin[nr] + own[nr]

            @pl.when(c < C - 1)
            def _():
                up_copy(nr, rin).start()

        @pl.when(jnp.logical_and(c < C - 1, jnp.logical_and(nl >= 0, nl < N)))
        def _():
            down_copy(nl, lin).wait_recv()
            lin[nl] = lin[nl] + own[nl]

            @pl.when(c > 0)
            def _():
                down_copy(nl, lin).start()

        @pl.when(m < I - i0)
        def _():
            strip_row(m + i0)

        @pl.when(jnp.logical_and(nf >= 0, nf < N))
        def _():
            i = i0 + nf // SPLIT
            h = lax.rem(nf, SPLIT)
            at = pl.ds(pl.multiple_of(h * H, H), H)
            k = i * R + r

            @pl.when(c == 0)
            def _():
                rbuf[i, at, :] = rbuf[i, at, :] - lin[nf]

            @pl.when(c == C - 1)
            def _():
                rbuf[i, at, :] = rbuf[i, at, :] - rin[nf]

            @pl.when(jnp.logical_and(c > 0, c < C - 1))
            def _():
                rbuf[i, at, :] = rbuf[i, at, :] - (rin[nf] + lin[nf] - own[nf])

            @pl.when(k < KS)
            def _():
                rbuf[i, at, :] = y[jnp.minimum(k, KS - 1), at, :]

            @pl.when(k == KS)
            def _():
                rbuf[i, at, :] = ps[at, :]

            @pl.when(h == SPLIT - 1)
            def _():
                f_copy(i).start()

        return carry

    lax.fori_loop(0, N + (C - 1) * SKEW, step, 0)

    for kind in range(KF + 2):
        z_wait_send(kind)
    drain((DG,) + bs + bk + ("tiles",) + cols)

    def flush(n, carry):
        @pl.when(c < C - 1)
        def _():
            up_copy(n, rin).wait_send()

        @pl.when(c > 0)
        def _():
            down_copy(n, lin).wait_send()

        return carry

    lax.fori_loop(0, N, flush, 0)
    pout.wait()

    def written(i, carry):
        f_copy(i).wait()
        strip_copy(i).wait()
        return carry

    lax.fori_loop(0, I, written, 0)


def per_device(panel, strip, factor, inv_diag, rhs):
    R = lax.axis_size("prow")
    C = lax.axis_size("pcol")
    A, TILE, _ = panel.shape
    I, _, CTD, _ = strip.shape
    KF = factor.shape[2]
    NR = rhs.shape[2]
    KS = KF * C
    assert KS <= R and R & (R - 1) == 0 and C % 2 == 0
    f32 = jnp.float32
    N = (I - KS // R) * SPLIT
    H = TILE // SPLIT
    bits = R.bit_length() - 1
    items = 2 * SPLIT + 1 + CTD + KS
    dma = pltpu.SemaphoreType.DMA
    panel_factor, new_strip, forward = pl.pallas_call(
        functools.partial(kernel, R, C, CTD, KF),
        out_shape=(
            jax.ShapeDtypeStruct(panel.shape, f32),
            jax.ShapeDtypeStruct((I, TILE * CTD, TILE), f32),
            jax.ShapeDtypeStruct(rhs.shape, f32),
        ),
        in_specs=[pl.BlockSpec(memory_space=pl.ANY)] * 5,
        out_specs=[pl.BlockSpec(memory_space=pl.ANY)] * 3,
        scratch_shapes=[
            pltpu.VMEM((I, TILE, TILE), f32),
            pltpu.VMEM((TILE, TILE), f32),
            pltpu.VMEM((CTD, TILE, TILE), f32),
            pltpu.VMEM((CTD, TILE, TILE), f32),
            pltpu.VMEM((TILE * KF, TILE), f32),
            pltpu.VMEM((KS + 1, KS, TILE, TILE), f32),
            pltpu.VMEM((KS + 1, TILE, NR), f32),
            pltpu.VMEM((KS, TILE, NR), f32),
            pltpu.VMEM((I, TILE * KF, TILE), f32),
            pltpu.VMEM((I, TILE, NR), f32),
            pltpu.VMEM((I, TILE * CTD, TILE), f32),
            pltpu.VMEM((KS, TILE, TILE), f32),
            pltpu.VMEM((N, H, NR), f32),
            pltpu.VMEM((N, H, NR), f32),
            pltpu.VMEM((N, H, NR), f32),
            pltpu.VMEM((A, TILE, TILE), f32),
            pltpu.VMEM((TILE, TILE), f32),
            pltpu.VMEM((TILE, TILE), f32),
            pltpu.VMEM((TILE, TILE), f32),
            pltpu.VMEM((TILE, NR), f32),
            dma((KF + 2, C - 1)),
            dma((KF + 2, C - 1)),
            dma((items, R // 2, bits)),
            dma((items, R)),
            dma((N,)),
            dma((N,)),
            dma((N,)),
            dma((N,)),
            dma((8,)),
            dma((I,)),
            dma((I,)),
            dma,
        ],
        compiler_params=pltpu.CompilerParams(
            collective_id=0, has_side_effects=True, vmem_limit_bytes=56 << 20
        ),
    )(
        panel,
        strip.reshape(I, TILE * CTD, TILE),
        factor.reshape(I, TILE * KF, TILE),
        inv_diag,
        rhs,
    )
    return panel_factor, new_strip.reshape(strip.shape), forward


def solution(mesh):
    in_specs = (
        P("pcol", "prow", None),
        P(None, "prow", None, "pcol"),
        P(None, "prow", None, "pcol"),
        P(),
        P(None, "prow", None),
    )
    out_specs = (P("pcol", "prow", None), P(None, "prow", None, "pcol"), P(None, "prow", None))
    return jax.shard_map(
        per_device, mesh=mesh, in_specs=in_specs, out_specs=out_specs, check_vma=False
    )
```

```python
import functools

import jax
import jax.numpy as jnp
from jax import lax
from jax.experimental import pallas as pl
from jax.experimental.pallas import tpu as pltpu
from jax.sharding import PartitionSpec as P

HIGHEST = lax.Precision.HIGHEST
HIGH = lax.Precision.HIGH
MESH = pl.DeviceIdType.MESH
SPLIT = 2
SKEW = 3


def dot(a, b, precision=HIGHEST):
    return jnp.dot(a, b, precision=precision, preferred_element_type=jnp.float32)


def when(cond, body):
    if cond is True:
        body()
    elif cond is not False:
        pl.when(cond)(body)


def flip(v, m):
    return v + m - 2 * m * lax.rem(lax.div(v, m), 2)


def copies(panel, strip, forward, panel_out, strip_out, forward_out, sem):
    pairs = ((forward, forward_out), (strip, strip_out), (panel, panel_out))
    made = [pltpu.make_async_copy(src, dst, sem.at[n]) for n, (src, dst) in enumerate(pairs)]
    for one in made:
        one.start()
    for one in made:
        one.wait()


def kernel(
    R, C, CTD, KF,
    panel, strip, factor, inv_diag, rhs,
    pbuf, sbuf, rbuf,
    pan_all, diag, col, colt, ftop, braw, dtile, ftri, brow, y, fbuf, own, rin, lin, tri, inv, inv_t, ps,
    z_send, z_recv, n_send, n_recv, p_send, p_recv, c_send, r_send, r_recv, l_send, l_recv, in_sem,
):
    r = lax.axis_index("prow")
    c = lax.axis_index("pcol")
    A, TILE, _ = panel.shape
    I = factor.shape[0]
    KS = KF * C
    full = KS == R
    i0 = KS // R
    H = TILE // SPLIT
    N = (I - i0) * SPLIT

    def target(row):
        return jnp.where(row == 0, KS, row) if full else row

    def slot(row):
        return target(row) if full else jnp.minimum(row, KS)

    def tiles_of(row):
        return target(row) if full else jnp.where(row <= KS, row, 0)

    first = jnp.where(r == 0, KS // R, 0) if full else 0
    b_own = True if full else r < KS
    k_own = r == KS % R
    mine = jnp.minimum(r, KS - 1)

    def load(n, src, dst):
        return pltpu.make_async_copy(src, dst, in_sem.at[n])

    loads = [
        load(0, panel, pan_all.at[pl.ds(c * A, A)]),
        load(1, factor.at[first], ftop),
        load(2, rhs.at[0], braw),
        load(3, rhs.at[KS // R], brow.at[KS]),
        load(4, inv_diag.at[mine], dtile),
        load(5, factor, fbuf),
        load(6, rhs, rbuf),
        load(7, strip, sbuf),
    ]
    conds = [True, True, b_own, k_own, True, True, True, True]
    for cond, one in zip(conds, loads):
        when(cond, one.start)

    dims = []
    m = 2
    while m < R:
        dims.append(m)
        m *= 2
    seqs = (dims + [1], dims[::-1] + [1])
    even = list(range(2, R, 2))

    def move(v, d):
        for m in seqs[0]:
            if d & m:
                v = flip(v, m)
        return v

    barrier = pltpu.get_barrier_semaphore()

    @pl.loop(1, C)
    def _(d):
        pl.semaphore_signal(barrier, inc=1, device_id={"pcol": lax.rem(c + d, C)}, device_id_type=MESH)

    for d in even + [1]:
        pl.semaphore_signal(barrier, inc=1, device_id={"prow": move(r, d)}, device_id_type=MESH)
    pl.semaphore_wait(barrier, C - 1 + len(even) + 1)

    DIA = KF
    dia_plane = KS // R // A

    def z_copy(kind, source, place):
        if kind is DIA:
            src, dst, at = pan_all.at[KS // R], diag, (KF, 0)
        else:
            src = dst = ftri.at[slot(r), kind * C + source]
            at = (kind, source)
        return pltpu.make_async_remote_copy(
            src_ref=src, dst_ref=dst, send_sem=z_send.at[at[0]], recv_sem=z_recv.at[at],
            device_id={"pcol": place}, device_id_type=MESH,
        )

    def z_cond(kind, source):
        if kind is DIA:
            return jnp.logical_and(k_own, source == dia_plane)
        return kind * C + source < tiles_of(r)

    def z_start(kind):
        @pl.when(z_cond(kind, c))
        def _():
            for d in range(1, C):
                z_copy(kind, c, lax.rem(c + d, C)).start()

    def z_wait_send(kind):
        @pl.when(z_cond(kind, c))
        def _():
            some = ftri.at[0, pl.ds(0, C - 1)]
            pltpu.make_async_remote_copy(
                src_ref=some, dst_ref=some, send_sem=z_send.at[kind], recv_sem=z_recv.at[0, 0],
                device_id={"pcol": c}, device_id_type=MESH,
            ).wait_send()

    def n_copy(source, way):
        ref = pan_all.at[pl.ds(source * A, A)]
        return pltpu.make_async_remote_copy(
            src_ref=ref, dst_ref=ref, send_sem=n_send.at[way, source], recv_sem=n_recv.at[source],
            device_id={"pcol": jnp.clip(c + (1 if way else -1), 0, C - 1)}, device_id_type=MESH,
        )

    def n_pass(dist):
        for way in (1, 0):
            source = c - dist if way else c + dist
            has = source >= 0 if way else source < C
            more = c < C - 1 if way else c > 0

            @pl.when(has)
            def _(way=way, source=source, more=more):
                if dist:
                    n_copy(source, way).wait_recv()

                @pl.when(more)
                def _():
                    n_copy(source, way).start()

    def n_done():
        @pl.loop(0, C)
        def _(source):
            @pl.when(jnp.logical_and(source <= c, c < C - 1))
            def _():
                n_copy(source, 1).wait_send()

            @pl.when(jnp.logical_and(source >= c, c > 0))
            def _():
                n_copy(source, 0).wait_send()

    B0, BK, DG, CL = 0, SPLIT, 2 * SPLIT, 2 * SPLIT + 1

    def wanted(s):
        return KS + 1 + s * C + c

    def place(kind, row):
        if kind < BK:
            return brow.at[jnp.minimum(row, KS - 1), pl.ds((kind - B0) * H, H)]
        if kind < DG:
            return brow.at[KS, pl.ds((kind - BK) * H, H)]
        if kind == DG:
            return diag
        return col.at[kind - CL]

    T0 = KS * SPLIT + SPLIT + 1 + CTD

    def p_index(kind, row):
        if kind < BK:
            return jnp.minimum(row, KS - 1) * SPLIT + kind
        return KS * SPLIT + kind - BK

    def t_index(j, row):
        t = slot(row)
        return T0 + lax.div(t * (t - 1), 2) + j

    def p_cond(kind, row):
        if kind < BK:
            return True if full else row < KS
        if kind <= DG:
            return row == KS % R
        return row == lax.rem(wanted(kind - CL), R)

    def order_of(kind):
        return 2 if kind >= DG else kind % 2

    def p_copy(index, ref, d, sem=None):
        return pltpu.make_async_remote_copy(
            src_ref=ref, dst_ref=ref, send_sem=p_send.at[0] if sem is None else sem, recv_sem=p_recv.at[index],
            device_id={"prow": move(r, d)}, device_id_type=MESH,
        )

    def outs(d, order):
        if order == 2:
            return [1] if d else even + [1]
        seq = seqs[order]
        at = max([n for n, m in enumerate(seq) if d & m], default=-1)
        return seq[at + 1:]

    def pass_on(index, ref, d, order, s=None):
        if d:
            p_copy(index, ref, 1).wait_recv()
        for m in outs(d, order):
            p_copy(index, ref, m, None if s is None else c_send.at[s, m // 2]).start()

    def spread(d, kinds):
        row = move(r, d)
        for kind in kinds:
            when(
                p_cond(kind, row),
                lambda kind=kind: pass_on(
                    p_index(kind, row), place(kind, row), d, order_of(kind), kind - CL if kind >= CL else None
                ),
            )

    def spread_tile(d, j, order):
        row = move(r, d)

        @pl.when(j < tiles_of(row))
        def _():
            pass_on(t_index(j, row), ftri.at[slot(row), j], d, order)

    def sent(k):
        total = 0
        for d in [0] + even:
            t = k ^ d
            count = [len(outs(d, order)) for order in range(3)]
            if t < KS:
                total += sum(count[n % 2] for n in range(SPLIT))
            if t == KS % R:
                total += sum(count[n % 2] for n in range(SPLIT)) + count[2]
            tiles = (KS if t == 0 else t) if full else (t if t <= KS else 0)
            total += sum(count[j % 2] for j in range(tiles))
        return total

    def drain():
        for k in range(R):
            if sent(k):
                @pl.when(r == k)
                def _(k=k):
                    whole, part = divmod(sent(k), KS)
                    for some in ([ftri.at[pl.ds(0, whole)]] if whole else []) + ([ftri.at[0, pl.ds(0, part)]] if part else []):
                        p_copy(0, some, 1).wait_send()
        for s in range(CTD):
            for d in [0] + even:
                @pl.when(p_cond(CL + s, move(r, d)))
                def _(s=s, d=d):
                    for m in outs(d, 2):
                        p_copy(0, col.at[s], m, c_send.at[s, m // 2]).wait_send()

    def odd(row, kinds, tiles=False):
        @pl.when(lax.rem(r + row, 2) == 1)
        def _():
            for kind in kinds:
                when(p_cond(kind, row), lambda kind=kind: p_copy(p_index(kind, row), place(kind, row), 1).wait_recv())
            if tiles:
                def one(j, carry):
                    p_copy(t_index(j, row), ftri.at[slot(row), j], 1).wait_recv()
                    return carry

                lax.fori_loop(0, tiles_of(row), one, 0)

    near = [d for d in even if d & (d - 1) == 0]
    far = [d for d in even if d & (d - 1) != 0]
    bs = tuple(range(B0, BK))
    bk = tuple(range(BK, DG))
    cols = tuple(range(CL, CL + CTD))

    loads[0].wait()
    z_start(DIA)

    @pl.when(z_cond(DIA, c))
    def _():
        diag[...] = pan_all[KS // R]
        spread(0, (DG,))

    loads[1].wait()
    loads[4].wait()
    for s in range(KF):
        @pl.when(z_cond(s, c))
        def _(s=s):
            own_tile = ftop[pl.ds(s, TILE, stride=KF), :]

            @pl.when(k_own)
            def _():
                ftri[slot(r), s * C + c] = own_tile

            @pl.when(jnp.logical_not(k_own))
            def _():
                ftri[slot(r), s * C + c] = dot(dtile[...], own_tile)

        z_start(s)

    @pl.when(jnp.logical_and(k_own, c != dia_plane))
    def _():
        z_copy(DIA, 0, c).wait_recv()
        spread(0, (DG,))

    when(k_own, loads[3].wait)

    def scale_rhs():
        loads[2].wait()
        brow[mine] = dot(dtile[...], braw[...])

    when(b_own, scale_rhs)
    spread(0, bs)

    def own_tiles(n, carry):
        for order in range(2):
            j = 2 * n + order
            source = lax.rem(j, C)

            @pl.when(jnp.logical_and(j < tiles_of(r), source != c))
            def _():
                at = (lax.div(j, C), source)
                ref = ftri.at[slot(r), j]
                pltpu.make_async_remote_copy(
                    src_ref=ref, dst_ref=ref, send_sem=z_send.at[0], recv_sem=z_recv.at[at],
                    device_id={"pcol": c}, device_id_type=MESH,
                ).wait_recv()

            spread_tile(0, j, order)
        return carry

    lax.fori_loop(0, KS // 2, own_tiles, 0)
    spread(0, bk)
    n_pass(0)

    for d in even:
        spread(d, (DG,))
    odd(KS % R, (DG,))

    lanes = lax.broadcasted_iota(jnp.int32, (TILE, TILE), 1)
    rows = lax.broadcasted_iota(jnp.int32, (TILE, TILE), 0)
    tri[...] = diag[...]
    inv[...] = jnp.where(lanes == rows, 1.0, 0.0)

    def eliminate(k, carry):
        lane = lanes[0:1]
        row = tri[pl.ds(k, 1), :]
        whole = tri[...]
        pivot = jnp.sum(jnp.where(lane == k, row, 0.0), axis=1, keepdims=True)
        scale = 1.0 / jnp.sqrt(pivot)
        lrow = jnp.where(lane >= k, row * scale, 0.0)
        column = jnp.sum(jnp.where(lanes == k, whole, 0.0), axis=1, keepdims=True)
        lcol = jnp.where(rows[:, 0:1] > k, column * scale, 0.0)
        wrow = inv[pl.ds(k, 1), :] * scale
        tri[...] = whole - lcol * lrow
        inv[...] = inv[...] - lcol * wrow
        tri[pl.ds(k, 1), :] = lrow
        inv[pl.ds(k, 1), :] = wrow
        return carry

    rounds = KS // 2 + 1
    count = 1 + 4 * rounds
    each = (TILE + count - 1) // count

    def part(n):
        lax.fori_loop(jnp.minimum(n * each, TILE), jnp.minimum((n + 1) * each, TILE), eliminate, 0)

    for d in near:
        spread(d, bs)
    part(0)
    for d in far:
        spread(d, bs)

    def relay(n, carry):
        for order in range(2):
            for d in near:
                spread_tile(d, 2 * n + order, order)
            part(1 + 4 * n + order)
        for order in range(2):
            for d in far:
                j = 2 * n - 2 + order

                @pl.when(j >= 0)
                def _(d=d, j=j, order=order):
                    spread_tile(d, j, order)

            part(3 + 4 * n + order)
        return carry

    lax.fori_loop(0, rounds, relay, 0)
    for d in near + far:
        spread(d, bk)
    inv_t[...] = inv[...].T
    n_pass(1)

    def arrived(t, carry):
        odd(t, bs)

        @pl.when(t > 0)
        def _():
            odd(t, (), True)

        return carry

    lax.fori_loop(0, KS, arrived, 0)
    for t in range(KS):
        total = brow[t]
        for j in range(t):
            total = total - dot(ftri[t, j], y[j], HIGH)
        y[t] = total


    def up_copy(n, src):
        return pltpu.make_async_remote_copy(
            src_ref=src.at[n], dst_ref=rin.at[n], send_sem=r_send.at[0], recv_sem=r_recv.at[n],
            device_id={"pcol": jnp.minimum(c + 1, C - 1)}, device_id_type=MESH,
        )

    def down_copy(n, src):
        return pltpu.make_async_remote_copy(
            src_ref=src.at[n], dst_ref=lin.at[n], send_sem=l_send.at[0], recv_sem=l_recv.at[n],
            device_id={"pcol": jnp.maximum(c - 1, 0)}, device_id_type=MESH,
        )

    loads[5].wait()

    def product(i, carry):
        total = dot(fbuf[i, pl.ds(0, TILE, stride=KF), :], y[c], HIGH)
        for s in range(1, KF):
            total = total + dot(fbuf[i, pl.ds(s, TILE, stride=KF), :], y[s * C + c], HIGH)
        for h in range(SPLIT):
            n = (i - i0) * SPLIT + h
            own[n] = total[h * H:(h + 1) * H]

            @pl.when(c == 0)
            def _():
                up_copy(n, own).start()

            @pl.when(c == C - 1)
            def _():
                down_copy(n, own).start()

        return carry

    lax.fori_loop(i0, I, product, 0)

    odd(KS % R, bk, True)
    rest = brow[KS]
    for j in range(KS):
        rest = rest - dot(ftri[KS, j], y[j], HIGH)
    ps[...] = dot(inv[...], rest)
    for dist in range(2, C - 1):
        n_pass(dist)
    for a in range(A):
        tile_a = (c * A + a) * R + r
        pbuf[a] = jnp.where(tile_a > KS, dot(pan_all[c * A + a], inv_t[...]), 0.0)

        @pl.when(tile_a == KS)
        def _(a=a):
            pbuf[a] = tri[...].T

    loads[6].wait()
    loads[7].wait()
    for i in range(i0):
        rbuf[i] = y[i * R + r]

    def strip_row(i):
        below = jnp.where(i * R + r > KS, dot(pan_all[i], inv_t[...], HIGH), 0.0)
        for s in range(CTD):
            at = pl.ds(s, TILE, stride=CTD)
            sbuf[i, at, :] = sbuf[i, at, :] - dot(below, colt[s], HIGH)
        rbuf[i] = rbuf[i] - dot(below, ps[...], HIGH)

    M = 4
    S0 = M + 5
    LAG = max((C - 1) * SKEW, S0 + 1)

    def step(m, carry):
        nr = m - c * SKEW
        nl = m - (C - 1 - c) * SKEW
        nf = m - LAG

        @pl.when(jnp.logical_and(c > 0, jnp.logical_and(nr >= 0, nr < N)))
        def _():
            up_copy(nr, rin).wait_recv()
            rin[nr] = rin[nr] + own[nr]

            @pl.when(c < C - 1)
            def _():
                up_copy(nr, rin).start()

        @pl.when(jnp.logical_and(c < C - 1, jnp.logical_and(nl >= 0, nl < N)))
        def _():
            down_copy(nl, lin).wait_recv()
            lin[nl] = lin[nl] + own[nl]

            @pl.when(c > 0)
            def _():
                down_copy(nl, lin).start()

        @pl.when(m == M)
        def _():
            n_pass(C - 1)
            for s in range(CTD):
                @pl.when(p_cond(CL + s, r))
                def _(s=s):
                    col[s] = pan_all[lax.div(wanted(s), R)]

            spread(0, cols)

        @pl.when(m == M + 2)
        def _():
            for d in even:
                spread(d, cols)

        @pl.when(m == M + 4)
        def _():
            for s in range(CTD):
                odd(lax.rem(wanted(s), R), (CL + s,))
            for s in range(CTD):
                colt[s] = dot(col[s], inv_t[...]).T

        @pl.when(jnp.logical_and(m >= S0, m < S0 + I - i0))
        def _():
            strip_row(m - S0 + i0)

        @pl.when(jnp.logical_and(nf >= 0, nf < N))
        def _():
            i = i0 + lax.div(nf, SPLIT)
            h = lax.rem(nf, SPLIT)
            at = pl.ds(pl.multiple_of(h * H, H), H)
            k = i * R + r

            @pl.when(c == 0)
            def _():
                rbuf[i, at, :] = rbuf[i, at, :] - lin[nf]

            @pl.when(c == C - 1)
            def _():
                rbuf[i, at, :] = rbuf[i, at, :] - rin[nf]

            @pl.when(jnp.logical_and(c > 0, c < C - 1))
            def _():
                rbuf[i, at, :] = rbuf[i, at, :] - (rin[nf] + lin[nf] - own[nf])

            @pl.when(k < KS)
            def _():
                rbuf[i, at, :] = y[jnp.minimum(k, KS - 1), at, :]

            @pl.when(k == KS)
            def _():
                rbuf[i, at, :] = ps[at, :]

        return carry

    lax.fori_loop(0, N + LAG, step, 0)

    for kind in range(KF):
        z_wait_send(kind)
    z_wait_send(DIA)
    n_done()
    drain()

    @pl.when(c < C - 1)
    def _():
        pltpu.make_async_remote_copy(
            src_ref=rin, dst_ref=rin, send_sem=r_send.at[0], recv_sem=r_recv.at[0],
            device_id={"pcol": c}, device_id_type=MESH,
        ).wait_send()

    @pl.when(c > 0)
    def _():
        pltpu.make_async_remote_copy(
            src_ref=lin, dst_ref=lin, send_sem=l_send.at[0], recv_sem=l_recv.at[0],
            device_id={"pcol": c}, device_id_type=MESH,
        ).wait_send()


def per_device(panel, strip, factor, inv_diag, rhs):
    R = lax.axis_size("prow")
    C = lax.axis_size("pcol")
    A, TILE, _ = panel.shape
    I, _, CTD, _ = strip.shape
    KF = factor.shape[2]
    NR = rhs.shape[2]
    KS = KF * C
    assert KS <= R and R & (R - 1) == 0 and KS % 2 == 0 and NR == SPLIT * TILE
    f32 = jnp.float32
    N = (I - KS // R) * SPLIT
    H = TILE // SPLIT
    bits = R.bit_length() - 1
    dma = pltpu.SemaphoreType.DMA
    shapes = (panel.shape, (I, TILE * CTD, TILE), rhs.shape)
    done = pl.pallas_call(
        functools.partial(kernel, R, C, CTD, KF),
        out_shape=[pltpu.VMEM(shape, f32) for shape in shapes],
        in_specs=[pl.BlockSpec(memory_space=pltpu.HBM)] * 5,
        out_specs=[pl.BlockSpec(memory_space=pltpu.VMEM)] * 3,
        scratch_shapes=[
            pltpu.VMEM((I, TILE, TILE), f32),
            pltpu.VMEM((TILE, TILE), f32),
            pltpu.VMEM((CTD, TILE, TILE), f32),
            pltpu.VMEM((CTD, TILE, TILE), f32),
            pltpu.VMEM((TILE * KF, TILE), f32),
            pltpu.VMEM((TILE, NR), f32),
            pltpu.VMEM((TILE, TILE), f32),
            pltpu.VMEM((KS + 1, KS, TILE, TILE), f32),
            pltpu.VMEM((KS + 1, TILE, NR), f32),
            pltpu.VMEM((KS, TILE, NR), f32),
            pltpu.VMEM((I, TILE * KF, TILE), f32),
            pltpu.VMEM((N, H, NR), f32),
            pltpu.VMEM((N, H, NR), f32),
            pltpu.VMEM((N, H, NR), f32),
            pltpu.VMEM((TILE, TILE), f32),
            pltpu.VMEM((TILE, TILE), f32),
            pltpu.VMEM((TILE, TILE), f32),
            pltpu.VMEM((TILE, NR), f32),
            dma((KF + 1,)),
            dma((KF + 1, C)),
            dma((2, C)),
            dma((C,)),
            dma((1,)),
            dma((KS * SPLIT + SPLIT + 1 + CTD + KS * (KS + 1) // 2,)),
            dma((CTD, R // 2)),
            dma((1,)),
            dma((N,)),
            dma((1,)),
            dma((N,)),
            dma((8,)),
        ],
        compiler_params=pltpu.CompilerParams(
            collective_id=0, has_side_effects=True, vmem_limit_bytes=44 << 20
        ),
    )(
        *(
            pltpu.with_memory_space_constraint(one, pltpu.HBM)
            for one in (
                panel,
                strip.reshape(I, TILE * CTD, TILE),
                factor.reshape(I, TILE * KF, TILE),
                inv_diag,
                rhs,
            )
        )
    )
    panel_factor, new_strip, forward = pl.pallas_call(
        copies,
        out_shape=[jax.ShapeDtypeStruct(shape, f32) for shape in shapes],
        in_specs=[pl.BlockSpec(memory_space=pltpu.VMEM)] * 3,
        out_specs=[pl.BlockSpec(memory_space=pl.ANY)] * 3,
        scratch_shapes=[dma((3,))],
        compiler_params=pltpu.CompilerParams(vmem_limit_bytes=16 << 20),
    )(*done)
    return panel_factor, new_strip.reshape(strip.shape), forward


def solution(mesh):
    in_specs = (
        P("pcol", "prow", None),
        P(None, "prow", None, "pcol"),
        P(None, "prow", None, "pcol"),
        P(),
        P(None, "prow", None),
    )
    out_specs = (P("pcol", "prow", None), P(None, "prow", None, "pcol"), P(None, "prow", None))
    return jax.shard_map(
        per_device, mesh=mesh, in_specs=in_specs, out_specs=out_specs, check_vma=False
    )
```

```python
import functools

import jax
import jax.numpy as jnp
from jax import lax
from jax.experimental import pallas as pl
from jax.experimental.pallas import tpu as pltpu
from jax.sharding import PartitionSpec as P

HIGHEST = lax.Precision.HIGHEST
HIGH = lax.Precision.HIGH
MESH = pl.DeviceIdType.MESH
SPLIT = 2
SKEW = 3
NB = 4


def dot(a, b, precision=HIGHEST):
    return jnp.dot(a, b, precision=precision, preferred_element_type=jnp.float32)


def when(cond, body):
    if cond is True:
        body()
    elif cond is not False:
        pl.when(cond)(body)


def flip(v, m):
    return v + m - 2 * m * lax.rem(lax.div(v, m), 2)


def copies(panel, strip, forward, panel_out, strip_out, forward_out, sem):
    pairs = ((forward, forward_out), (strip, strip_out), (panel, panel_out))
    made = [pltpu.make_async_copy(src, dst, sem.at[n]) for n, (src, dst) in enumerate(pairs)]
    for one in made:
        one.start()
    for one in made:
        one.wait()


def kernel(
    R, C, CTD, KF,
    panel, strip, factor, inv_diag, rhs,
    pbuf, sbuf, rbuf,
    pan_all, diag, col, colt, ftop, braw, dtile, ftri, brow, y, fbuf, own, rin, lin, tri, inv, inv_t, ps, rest,
    z_send, z_recv, n_send, n_recv, p_send, p_recv, c_send, r_send, r_recv, l_send, l_recv, in_sem,
):
    r = lax.axis_index("prow")
    c = lax.axis_index("pcol")
    A, TILE, _ = panel.shape
    I = factor.shape[0]
    KS = KF * C
    full = KS == R
    i0 = KS // R
    H = TILE // SPLIT
    N = (I - i0) * SPLIT

    def slot(row):
        return jnp.minimum(row, KS - 1)

    def tiles_of(row):
        return jnp.where(row < KS, row, 0)

    b_own = True if full else r < KS
    k_own = r == KS % R
    mine = jnp.minimum(r, KS - 1)

    def load(n, src, dst):
        return pltpu.make_async_copy(src, dst, in_sem.at[n])

    loads = [
        load(0, panel, pan_all.at[pl.ds(c * A, A)]),
        load(1, factor.at[0], ftop),
        load(2, rhs.at[0], braw),
        load(3, inv_diag.at[mine], dtile),
        load(4, factor, fbuf),
        load(5, rhs, rbuf),
        load(6, strip, sbuf),
    ]
    conds = [True, True, b_own, True, True, True, True]
    for cond, one in zip(conds, loads):
        when(cond, one.start)

    dims = []
    m = 2
    while m < R:
        dims.append(m)
        m *= 2
    seqs = (dims + [1], dims[::-1] + [1])
    even = list(range(2, R, 2))

    def move(v, d):
        for m in seqs[0]:
            if d & m:
                v = flip(v, m)
        return v

    barrier = pltpu.get_barrier_semaphore()

    @pl.loop(1, C)
    def _(d):
        pl.semaphore_signal(barrier, inc=1, device_id={"pcol": lax.rem(c + d, C)}, device_id_type=MESH)

    for d in even + [1]:
        pl.semaphore_signal(barrier, inc=1, device_id={"prow": move(r, d)}, device_id_type=MESH)
    pl.semaphore_wait(barrier, C - 1 + len(even) + 1)

    DIA = KF
    dia_plane = KS // R // A

    def z_copy(kind, source, place):
        if kind is DIA:
            src, dst, at = pan_all.at[KS // R], diag, (KF, 0)
        else:
            src = dst = ftri.at[slot(r), kind * C + source]
            at = (kind, source)
        return pltpu.make_async_remote_copy(
            src_ref=src, dst_ref=dst, send_sem=z_send.at[at[0]], recv_sem=z_recv.at[at],
            device_id={"pcol": place}, device_id_type=MESH,
        )

    def z_cond(kind, source):
        if kind is DIA:
            return jnp.logical_and(k_own, source == dia_plane)
        return kind * C + source < tiles_of(r)

    def z_start(kind):
        @pl.when(z_cond(kind, c))
        def _():
            for d in range(1, C):
                z_copy(kind, c, lax.rem(c + d, C)).start()

    def z_wait_send(kind):
        @pl.when(z_cond(kind, c))
        def _():
            some = ftri.at[0, pl.ds(0, C - 1)]
            pltpu.make_async_remote_copy(
                src_ref=some, dst_ref=some, send_sem=z_send.at[kind], recv_sem=z_recv.at[0, 0],
                device_id={"pcol": c}, device_id_type=MESH,
            ).wait_send()

    def n_copy(source, way):
        ref = pan_all.at[pl.ds(source * A, A)]
        return pltpu.make_async_remote_copy(
            src_ref=ref, dst_ref=ref, send_sem=n_send.at[way, source], recv_sem=n_recv.at[source],
            device_id={"pcol": jnp.clip(c + (1 if way else -1), 0, C - 1)}, device_id_type=MESH,
        )

    def n_pass(dist):
        for way in (1, 0):
            source = c - dist if way else c + dist
            has = source >= 0 if way else source < C
            more = c < C - 1 if way else c > 0

            @pl.when(has)
            def _(way=way, source=source, more=more):
                if dist:
                    n_copy(source, way).wait_recv()

                @pl.when(more)
                def _():
                    n_copy(source, way).start()

    def n_done():
        @pl.loop(0, C)
        def _(source):
            @pl.when(jnp.logical_and(source <= c, c < C - 1))
            def _():
                n_copy(source, 1).wait_send()

            @pl.when(jnp.logical_and(source >= c, c > 0))
            def _():
                n_copy(source, 0).wait_send()

    DG, PS, CL = SPLIT, SPLIT + 1, 2 * SPLIT + 1

    def wanted(s):
        return KS + 1 + s * C + c

    def place(kind, row):
        if kind < DG:
            return brow.at[slot(row), pl.ds(kind * H, H)]
        if kind == DG:
            return diag
        if kind < CL:
            return ps.at[pl.ds((kind - PS) * H, H)]
        return col.at[kind - CL]

    T0 = KS * SPLIT + 1 + SPLIT + CTD

    def p_index(kind, row):
        if kind < DG:
            return slot(row) * SPLIT + kind
        return KS * SPLIT + kind - DG

    def t_index(j, row):
        return T0 + lax.div(row * (row - 1), 2) + j

    def p_cond(kind, row):
        if kind < DG:
            return True if full else row < KS
        if kind < CL:
            return row == KS % R
        return row == lax.rem(wanted(kind - CL), R)

    def in_order(row, j, order):
        last = row >= 3 * R // 4
        odd_one = lax.rem(j, 2) == 1
        high = jnp.logical_and(row >= R // 2, jnp.logical_not(jnp.logical_and(last, odd_one)))
        return high if order else jnp.logical_not(high)

    def nth(q):
        k = lax.div(q, KF)
        away = jnp.where(lax.rem(k, 2) == 1, lax.div(k + 1, 2), C - lax.div(k, 2))
        return lax.rem(q, KF) * C + lax.rem(c + away, C)

    def p_copy(index, ref, d, sem=None):
        return pltpu.make_async_remote_copy(
            src_ref=ref, dst_ref=ref, send_sem=p_send.at[0] if sem is None else sem, recv_sem=p_recv.at[index],
            device_id={"prow": move(r, d)}, device_id_type=MESH,
        )

    def outs(d, order):
        if order == 2:
            return [1] if d else even + [1]
        seq = seqs[order]
        at = max([n for n, m in enumerate(seq) if d & m], default=-1)
        return seq[at + 1:]

    def pass_on(index, ref, d, order, s=None):
        if d:
            p_copy(index, ref, 1).wait_recv()
        for m in outs(d, order):
            p_copy(index, ref, m, None if s is None else c_send.at[s, m // 2]).start()

    def spread(d, kinds):
        row = move(r, d)
        for kind in kinds:
            @pl.when(p_cond(kind, row))
            def _(kind=kind):
                ref = place(kind, row)
                if kind >= DG:
                    pass_on(p_index(kind, row), ref, d, 2, kind - PS if kind > DG else None)
                else:
                    for order in range(2):
                        @pl.when(in_order(row, kind, order))
                        def _(order=order):
                            pass_on(p_index(kind, row), ref, d, order)

    def spread_tile(d, q):
        row = move(r, d)
        j = nth(q)

        @pl.when(j < tiles_of(row))
        def _():
            for order in range(2):
                @pl.when(in_order(row, j, order))
                def _(order=order):
                    pass_on(t_index(j, row), ftri.at[slot(row), j], d, order)

    def sent(k):
        total = 0
        for d in [0] + even:
            t = k ^ d

            def count(j):
                high = t >= R // 2 and not (t >= 3 * R // 4 and j % 2 == 1)
                return len(outs(d, int(high)))

            if t < KS:
                total += sum(count(n) for n in range(SPLIT)) + sum(count(j) for j in range(t))
            if t == KS % R:
                total += len(outs(d, 2))
        return total

    def drain():
        for k in range(R):
            if sent(k):
                @pl.when(r == k)
                def _(k=k):
                    whole, part = divmod(sent(k), KS)
                    for some in ([ftri.at[pl.ds(0, whole)]] if whole else []) + ([ftri.at[0, pl.ds(0, part)]] if part else []):
                        p_copy(0, some, 1).wait_send()
        for kind in psol + cols:
            for d in [0] + even:
                @pl.when(p_cond(kind, move(r, d)))
                def _(kind=kind, d=d):
                    for m in outs(d, 2):
                        p_copy(0, place(kind, KS % R), m, c_send.at[kind - PS, m // 2]).wait_send()

    def odd(row, kinds, tiles=False):
        @pl.when(lax.rem(r + row, 2) == 1)
        def _():
            for kind in kinds:
                when(p_cond(kind, row), lambda kind=kind: p_copy(p_index(kind, row), place(kind, row), 1).wait_recv())
            if tiles:
                def one(j, carry):
                    p_copy(t_index(j, row), ftri.at[slot(row), j], 1).wait_recv()
                    return carry

                lax.fori_loop(0, tiles_of(row), one, 0)

    near = [d for d in even if d & (d - 1) == 0]
    far = [d for d in even if d & (d - 1) != 0]
    bs = tuple(range(DG))
    psol = tuple(range(PS, CL))
    cols = tuple(range(CL, CL + CTD))

    loads[0].wait()
    z_start(DIA)

    @pl.when(z_cond(DIA, c))
    def _():
        diag[...] = pan_all[KS // R]
        spread(0, (DG,))

    loads[1].wait()
    loads[3].wait()
    for s in range(KF):
        @pl.when(z_cond(s, c))
        def _(s=s):
            ftri[slot(r), s * C + c] = dot(dtile[...], ftop[pl.ds(s, TILE, stride=KF), :])

        z_start(s)

    @pl.when(jnp.logical_and(k_own, c != dia_plane))
    def _():
        z_copy(DIA, 0, c).wait_recv()
        spread(0, (DG,))


    def scale_rhs():
        loads[2].wait()
        brow[mine] = dot(dtile[...], braw[...])

    when(b_own, scale_rhs)
    spread(0, bs)

    def own_tile(q, carry):
        j = nth(q)
        source = lax.rem(j, C)

        @pl.when(jnp.logical_and(j < tiles_of(r), source != c))
        def _():
            ref = ftri.at[slot(r), j]
            pltpu.make_async_remote_copy(
                src_ref=ref, dst_ref=ref, send_sem=z_send.at[0], recv_sem=z_recv.at[lax.div(j, C), source],
                device_id={"pcol": c}, device_id_type=MESH,
            ).wait_recv()

        spread_tile(0, q)
        return carry

    lax.fori_loop(0, KS, own_tile, 0)
    n_pass(0)

    for d in even:
        spread(d, (DG,))
    odd(KS % R, (DG,))

    lanes = lax.broadcasted_iota(jnp.int32, (TILE, TILE), 1)
    rows = lax.broadcasted_iota(jnp.int32, (TILE, TILE), 0)
    tri[...] = diag[...]
    inv[...] = jnp.where(lanes == rows, 1.0, 0.0)

    lane = lanes[0:1]
    at_row = rows[:, 0:1]

    def pick(mask, values):
        return jnp.sum(jnp.where(mask, values, 0.0), axis=1, keepdims=True)

    def eliminate(b, carry):
        k = b * NB
        whole = tri[...]
        row = [tri[pl.ds(k + i, 1), :] for i in range(NB)]
        wrow = [inv[pl.ds(k + i, 1), :] for i in range(NB)]
        column = [pick(lanes == k + i, whole) for i in range(NB)]
        pivot = [[pick(lane == k + j, row[i]) if j >= i else None for j in range(NB)] for i in range(NB)]
        for i in range(NB):
            for h in range(i):
                factor_hi = pivot[h][i]
                for j in range(i, NB):
                    pivot[i][j] = pivot[i][j] - factor_hi * pivot[h][j]
                row[i] = row[i] - factor_hi * row[h]
                wrow[i] = wrow[i] - factor_hi * wrow[h]
                column[i] = column[i] - factor_hi * column[h]
            scale = 1.0 / jnp.sqrt(pivot[i][i])
            for j in range(i, NB):
                pivot[i][j] = pivot[i][j] * scale
            row[i] = jnp.where(lane >= k + i, row[i] * scale, 0.0)
            wrow[i] = wrow[i] * scale
            column[i] = column[i] * scale
        rest = inv[...]
        for i in range(NB):
            lcol = jnp.where(at_row > k + NB - 1, column[i], 0.0)
            whole = whole - lcol * row[i]
            rest = rest - lcol * wrow[i]
        tri[...] = whole
        inv[...] = rest
        for i in range(NB):
            tri[pl.ds(k + i, 1), :] = row[i]
            inv[pl.ds(k + i, 1), :] = wrow[i]
        return carry

    rounds = KS // 2 + 1
    count = 1 + 4 * rounds
    blocks = TILE // NB
    each = (blocks + count - 1) // count

    def part(n):
        lax.fori_loop(jnp.minimum(n * each, blocks), jnp.minimum((n + 1) * each, blocks), eliminate, 0)

    for d in near:
        spread(d, bs)
    part(0)
    for d in far:
        spread(d, bs)

    def relay(n, carry):
        for p in range(2):
            for d in near:
                @pl.when(n < rounds - 1)
                def _(d=d, p=p):
                    spread_tile(d, 2 * n + p)
            part(1 + 4 * n + p)
        for p in range(2):
            for d in far:
                @pl.when(n > 0)
                def _(d=d, p=p):
                    spread_tile(d, 2 * n - 2 + p)

            part(3 + 4 * n + p)
        return carry

    lax.fori_loop(0, rounds, relay, 0)
    inv_t[...] = inv[...].T
    n_pass(1)

    def arrived(t, carry):
        odd(t, bs)

        @pl.when(t > 0)
        def _():
            odd(t, (), True)

        return carry

    lax.fori_loop(0, KS, arrived, 0)
    for t in range(KS):
        total = brow[t]
        for j in range(t):
            total = total - dot(ftri[t, j], y[j], HIGH)
        y[t] = total


    def up_copy(n, src):
        return pltpu.make_async_remote_copy(
            src_ref=src.at[n], dst_ref=rin.at[n], send_sem=r_send.at[0], recv_sem=r_recv.at[n],
            device_id={"pcol": jnp.minimum(c + 1, C - 1)}, device_id_type=MESH,
        )

    def down_copy(n, src):
        return pltpu.make_async_remote_copy(
            src_ref=src.at[n], dst_ref=lin.at[n], send_sem=l_send.at[0], recv_sem=l_recv.at[n],
            device_id={"pcol": jnp.maximum(c - 1, 0)}, device_id_type=MESH,
        )

    loads[4].wait()

    def product(i):
        total = dot(fbuf[i, pl.ds(0, TILE, stride=KF), :], y[c], HIGH)
        for s in range(1, KF):
            total = total + dot(fbuf[i, pl.ds(s, TILE, stride=KF), :], y[s * C + c], HIGH)
        for h in range(SPLIT):
            n = (i - i0) * SPLIT + h
            own[n] = total[h * H:(h + 1) * H]

            @pl.when(c == 0)
            def _():
                up_copy(n, own).start()

            @pl.when(c == C - 1)
            def _():
                down_copy(n, own).start()

    for dist in range(2, C - 1):
        n_pass(dist)
    loads[5].wait()
    loads[6].wait()
    for i in range(i0):
        rbuf[i] = y[i * R + r]

    def strip_row(i):
        below = jnp.where(i * R + r > KS, dot(pan_all[i], inv_t[...], HIGH), 0.0)
        for s in range(CTD):
            at = pl.ds(s, TILE, stride=CTD)
            sbuf[i, at, :] = sbuf[i, at, :] - dot(below, colt[s], HIGH)
        rbuf[i] = rbuf[i] - dot(below, ps[...], HIGH)

    def total(n):
        return jnp.where(c == 0, lin[n], jnp.where(c == C - 1, rin[n], rin[n] + lin[n] - own[n]))

    def assemble(n, carry):
        i = i0 + lax.div(n, SPLIT)
        at = pl.ds(pl.multiple_of(lax.rem(n, SPLIT) * H, H), H)
        k = i * R + r
        rbuf[i, at, :] = rbuf[i, at, :] - total(n)

        @pl.when(k < KS)
        def _():
            rbuf[i, at, :] = y[slot(k), at, :]

        @pl.when(k == KS)
        def _():
            rbuf[i, at, :] = ps[at, :]

        return carry

    M = 4
    far_lag = (C - 1) * SKEW
    P0 = far_lag + SPLIT - 1
    S0 = P0 + 5
    ROWS = 2

    def rows_done(m):
        return jnp.clip(ROWS * (m - S0 + 1), 0, I - i0)

    def chunks_done(m):
        return jnp.clip(jnp.minimum(m - far_lag + 1, SPLIT * rows_done(m)), 0, N)

    def step(m, carry):
        nr = m - c * SKEW
        nl = m - (C - 1 - c) * SKEW

        @pl.when(m < I - i0)
        def _():
            product(m + i0)

        @pl.when(jnp.logical_and(c > 0, jnp.logical_and(nr >= 0, nr < N)))
        def _():
            up_copy(nr, rin).wait_recv()

            @pl.when(c < C - 1)
            def _():
                rin[nr] = rin[nr] + own[nr]
                up_copy(nr, rin).start()

            @pl.when(c == C - 1)
            def _():
                rin[nr] = rin[nr] + own[nr]

        @pl.when(jnp.logical_and(c < C - 1, jnp.logical_and(nl >= 0, nl < N)))
        def _():
            down_copy(nl, lin).wait_recv()
            lin[nl] = lin[nl] + own[nl]

            @pl.when(c > 0)
            def _():
                down_copy(nl, lin).start()

        @pl.when(m == M)
        def _():
            n_pass(C - 1)
            for s in range(CTD):
                @pl.when(p_cond(CL + s, r))
                def _(s=s):
                    col[s] = pan_all[lax.div(wanted(s), R)]

            spread(0, cols)

        @pl.when(m == M + 2)
        def _():
            for d in even:
                spread(d, cols)

        @pl.when(m == M + 3)
        def _():
            for a in range(A):
                tile_a = (c * A + a) * R + r
                pbuf[a] = jnp.where(tile_a > KS, dot(pan_all[c * A + a], inv_t[...]), 0.0)

                @pl.when(tile_a == KS)
                def _(a=a):
                    pbuf[a] = tri[...].T

        @pl.when(m == M + 4)
        def _():
            for s in range(CTD):
                odd(lax.rem(wanted(s), R), (CL + s,))
            for s in range(CTD):
                colt[s] = dot(col[s], inv_t[...]).T

        @pl.when(jnp.logical_and(m == P0, k_own))
        def _():
            for h in range(SPLIT):
                rest[pl.ds(h * H, H), :] = rbuf[i0, pl.ds(h * H, H), :] - total(h)
            ps[...] = dot(inv[...], rest[...])
            spread(0, psol)

        @pl.when(m == P0 + 3)
        def _():
            for d in even:
                spread(d, psol)

        @pl.when(m == P0 + 4)
        def _():
            odd(KS % R, psol)

        def one_row(n, carry):
            strip_row(n + i0)
            return carry

        lax.fori_loop(rows_done(m - 1), rows_done(m), one_row, 0)
        lax.fori_loop(chunks_done(m - 1), chunks_done(m), assemble, 0)
        return carry

    lax.fori_loop(0, N + far_lag, step, 0)

    for kind in range(KF):
        z_wait_send(kind)
    z_wait_send(DIA)
    n_done()
    drain()

    @pl.when(c < C - 1)
    def _():
        pltpu.make_async_remote_copy(
            src_ref=rin, dst_ref=rin, send_sem=r_send.at[0], recv_sem=r_recv.at[0],
            device_id={"pcol": c}, device_id_type=MESH,
        ).wait_send()

    @pl.when(c > 0)
    def _():
        pltpu.make_async_remote_copy(
            src_ref=lin, dst_ref=lin, send_sem=l_send.at[0], recv_sem=l_recv.at[0],
            device_id={"pcol": c}, device_id_type=MESH,
        ).wait_send()


def per_device(panel, strip, factor, inv_diag, rhs):
    R = lax.axis_size("prow")
    C = lax.axis_size("pcol")
    A, TILE, _ = panel.shape
    I, _, CTD, _ = strip.shape
    KF = factor.shape[2]
    NR = rhs.shape[2]
    KS = KF * C
    assert KS <= R and R & (R - 1) == 0 and KS % 2 == 0 and NR == SPLIT * TILE
    f32 = jnp.float32
    N = (I - KS // R) * SPLIT
    H = TILE // SPLIT
    bits = R.bit_length() - 1
    dma = pltpu.SemaphoreType.DMA
    shapes = (panel.shape, (I, TILE * CTD, TILE), rhs.shape)
    done = pl.pallas_call(
        functools.partial(kernel, R, C, CTD, KF),
        out_shape=[pltpu.VMEM(shape, f32) for shape in shapes],
        in_specs=[pl.BlockSpec(memory_space=pltpu.HBM)] * 5,
        out_specs=[pl.BlockSpec(memory_space=pltpu.VMEM)] * 3,
        scratch_shapes=[
            pltpu.VMEM((I, TILE, TILE), f32),
            pltpu.VMEM((TILE, TILE), f32),
            pltpu.VMEM((CTD, TILE, TILE), f32),
            pltpu.VMEM((CTD, TILE, TILE), f32),
            pltpu.VMEM((TILE * KF, TILE), f32),
            pltpu.VMEM((TILE, NR), f32),
            pltpu.VMEM((TILE, TILE), f32),
            pltpu.VMEM((KS, KS, TILE, TILE), f32),
            pltpu.VMEM((KS, TILE, NR), f32),
            pltpu.VMEM((KS, TILE, NR), f32),
            pltpu.VMEM((I, TILE * KF, TILE), f32),
            pltpu.VMEM((N, H, NR), f32),
            pltpu.VMEM((N, H, NR), f32),
            pltpu.VMEM((N, H, NR), f32),
            pltpu.VMEM((TILE, TILE), f32),
            pltpu.VMEM((TILE, TILE), f32),
            pltpu.VMEM((TILE, TILE), f32),
            pltpu.VMEM((TILE, NR), f32),
            pltpu.VMEM((TILE, NR), f32),
            dma((KF + 1,)),
            dma((KF + 1, C)),
            dma((2, C)),
            dma((C,)),
            dma((1,)),
            dma((KS * SPLIT + 1 + SPLIT + CTD + KS * (KS - 1) // 2,)),
            dma((SPLIT + CTD, R // 2)),
            dma((1,)),
            dma((N,)),
            dma((1,)),
            dma((N,)),
            dma((7,)),
        ],
        compiler_params=pltpu.CompilerParams(
            collective_id=0, has_side_effects=True, vmem_limit_bytes=44 << 20
        ),
    )(
        *(
            pltpu.with_memory_space_constraint(one, pltpu.HBM)
            for one in (
                panel,
                strip.reshape(I, TILE * CTD, TILE),
                factor.reshape(I, TILE * KF, TILE),
                inv_diag,
                rhs,
            )
        )
    )
    panel_factor, new_strip, forward = pl.pallas_call(
        copies,
        out_shape=[jax.ShapeDtypeStruct(shape, f32) for shape in shapes],
        in_specs=[pl.BlockSpec(memory_space=pltpu.VMEM)] * 3,
        out_specs=[pl.BlockSpec(memory_space=pl.ANY)] * 3,
        scratch_shapes=[dma((3,))],
        compiler_params=pltpu.CompilerParams(vmem_limit_bytes=16 << 20),
    )(*done)
    return panel_factor, new_strip.reshape(strip.shape), forward


def solution(mesh):
    in_specs = (
        P("pcol", "prow", None),
        P(None, "prow", None, "pcol"),
        P(None, "prow", None, "pcol"),
        P(),
        P(None, "prow", None),
    )
    out_specs = (P("pcol", "prow", None), P(None, "prow", None, "pcol"), P(None, "prow", None))
    return jax.shard_map(
        per_device, mesh=mesh, in_specs=in_specs, out_specs=out_specs, check_vma=False
    )
```

```python
import functools

import jax
import jax.numpy as jnp
from jax import lax
from jax.experimental import pallas as pl
from jax.experimental.pallas import tpu as pltpu
from jax.sharding import PartitionSpec as P

HIGHEST = lax.Precision.HIGHEST
HIGH = lax.Precision.HIGH
MESH = pl.DeviceIdType.MESH
SPLIT = 2
EARLY_TILES = 1
SKEW = 3
NB = 4


def dot(a, b, precision=HIGHEST):
    return jnp.dot(a, b, precision=precision, preferred_element_type=jnp.float32)


def when(cond, body):
    if cond is True:
        body()
    elif cond is not False:
        pl.when(cond)(body)


def flip(v, m):
    return v + m - 2 * m * lax.rem(lax.div(v, m), 2)


def copies(panel, strip, forward, panel_out, strip_out, forward_out, sem):
    pairs = ((forward, forward_out), (strip, strip_out), (panel, panel_out))
    made = [pltpu.make_async_copy(src, dst, sem.at[n]) for n, (src, dst) in enumerate(pairs)]
    for one in made:
        one.start()
    for one in made:
        one.wait()


def kernel(
    R, C, CTD, KF,
    panel, strip, factor, inv_diag, rhs,
    pbuf, sbuf, rbuf,
    pan_all, diag, col, colt, ftop, braw, dtile, ftri, brow, y, fbuf, xbuf, own, rin, lin, tri, inv, inv_t, ps, rest,
    z_send, z_recv, n_send, n_recv, p_send, p_recv, c_send, x_send, x_recv, r_send, r_recv, l_send, l_recv, in_sem,
):
    r = lax.axis_index("prow")
    c = lax.axis_index("pcol")
    A, TILE, _ = panel.shape
    I = factor.shape[0]
    KS = KF * C
    full = KS == R
    i0 = KS // R
    H = TILE // SPLIT
    N = (I - i0) * SPLIT
    EARLY = xbuf.shape[1]
    NS = N - EARLY * SPLIT

    def slot(row):
        return jnp.minimum(row, KS - 1)

    def tiles_of(row):
        return jnp.where(row < KS, row, 0)

    b_own = True if full else r < KS
    k_own = r == KS % R
    mine = jnp.minimum(r, KS - 1)

    def load(n, src, dst):
        return pltpu.make_async_copy(src, dst, in_sem.at[n])

    loads = [
        load(0, panel, pan_all.at[pl.ds(c * A, A)]),
        load(1, factor.at[0], ftop),
        load(2, rhs.at[0], braw),
        load(3, inv_diag.at[mine], dtile),
        load(4, factor, fbuf),
        load(5, rhs, rbuf),
        load(6, strip, sbuf),
    ]
    conds = [True, True, b_own, True, True, True, True]
    for cond, one in zip(conds, loads):
        when(cond, one.start)

    dims = []
    m = 2
    while m < R:
        dims.append(m)
        m *= 2
    seqs = (dims + [1], dims[::-1] + [1])
    even = list(range(2, R, 2))

    def move(v, d):
        for m in seqs[0]:
            if d & m:
                v = flip(v, m)
        return v

    barrier = pltpu.get_barrier_semaphore()

    @pl.loop(1, C)
    def _(d):
        pl.semaphore_signal(barrier, inc=1, device_id={"pcol": lax.rem(c + d, C)}, device_id_type=MESH)

    for d in even + [1]:
        pl.semaphore_signal(barrier, inc=1, device_id={"prow": move(r, d)}, device_id_type=MESH)
    pl.semaphore_wait(barrier, C - 1 + len(even) + 1)

    DIA = KF
    dia_plane = KS // R // A

    def z_copy(kind, source, place):
        if kind is DIA:
            src, dst, at = pan_all.at[KS // R], diag, (KF, 0)
        else:
            src = dst = ftri.at[slot(r), kind * C + source]
            at = (kind, source)
        return pltpu.make_async_remote_copy(
            src_ref=src, dst_ref=dst, send_sem=z_send.at[at[0]], recv_sem=z_recv.at[at],
            device_id={"pcol": place}, device_id_type=MESH,
        )

    def z_cond(kind, source):
        if kind is DIA:
            return jnp.logical_and(k_own, source == dia_plane)
        return kind * C + source < tiles_of(r)

    def z_start(kind):
        @pl.when(z_cond(kind, c))
        def _():
            for d in range(1, C):
                z_copy(kind, c, lax.rem(c + d, C)).start()

    def z_wait_send(kind):
        @pl.when(z_cond(kind, c))
        def _():
            some = ftri.at[0, pl.ds(0, C - 1)]
            pltpu.make_async_remote_copy(
                src_ref=some, dst_ref=some, send_sem=z_send.at[kind], recv_sem=z_recv.at[0, 0],
                device_id={"pcol": c}, device_id_type=MESH,
            ).wait_send()

    def n_copy(source, way):
        ref = pan_all.at[pl.ds(source * A, A)]
        return pltpu.make_async_remote_copy(
            src_ref=ref, dst_ref=ref, send_sem=n_send.at[way, source], recv_sem=n_recv.at[source],
            device_id={"pcol": jnp.clip(c + (1 if way else -1), 0, C - 1)}, device_id_type=MESH,
        )

    def n_pass(dist):
        for way in (1, 0):
            source = c - dist if way else c + dist
            has = source >= 0 if way else source < C
            more = c < C - 1 if way else c > 0

            @pl.when(has)
            def _(way=way, source=source, more=more):
                if dist:
                    n_copy(source, way).wait_recv()

                @pl.when(more)
                def _():
                    n_copy(source, way).start()

    def n_done():
        @pl.loop(0, C)
        def _(source):
            @pl.when(jnp.logical_and(source <= c, c < C - 1))
            def _():
                n_copy(source, 1).wait_send()

            @pl.when(jnp.logical_and(source >= c, c > 0))
            def _():
                n_copy(source, 0).wait_send()

    DG, PS, CL = SPLIT, SPLIT + 1, 2 * SPLIT + 1

    def wanted(s):
        return KS + 1 + s * C + c

    def place(kind, row):
        if kind < DG:
            return brow.at[slot(row), pl.ds(kind * H, H)]
        if kind == DG:
            return diag
        if kind < CL:
            return ps.at[pl.ds((kind - PS) * H, H)]
        return col.at[kind - CL]

    T0 = KS * SPLIT + 1 + SPLIT + CTD

    def p_index(kind, row):
        if kind < DG:
            return slot(row) * SPLIT + kind
        return KS * SPLIT + kind - DG

    def t_index(j, row):
        return T0 + lax.div(row * (row - 1), 2) + j

    def p_cond(kind, row):
        if kind < DG:
            return True if full else row < KS
        if kind < CL:
            return row == KS % R
        return row == lax.rem(wanted(kind - CL), R)

    def in_order(row, j, order):
        last = row >= 3 * R // 4
        odd_one = lax.rem(j, 2) == 1
        high = jnp.logical_and(row >= R // 2, jnp.logical_not(jnp.logical_and(last, odd_one)))
        return high if order else jnp.logical_not(high)

    def nth(q):
        k = lax.div(q, KF)
        away = jnp.where(lax.rem(k, 2) == 1, lax.div(k + 1, 2), C - lax.div(k, 2))
        return lax.rem(q, KF) * C + lax.rem(c + away, C)

    def p_copy(index, ref, d, sem=None):
        return pltpu.make_async_remote_copy(
            src_ref=ref, dst_ref=ref, send_sem=p_send.at[0] if sem is None else sem, recv_sem=p_recv.at[index],
            device_id={"prow": move(r, d)}, device_id_type=MESH,
        )

    def outs(d, order):
        if order == 2:
            return [1] if d else even + [1]
        seq = seqs[order]
        at = max([n for n, m in enumerate(seq) if d & m], default=-1)
        return seq[at + 1:]

    def pass_on(index, ref, d, order, s=None):
        if d:
            p_copy(index, ref, 1).wait_recv()
        for m in outs(d, order):
            p_copy(index, ref, m, None if s is None else c_send.at[s, m // 2]).start()

    def spread(d, kinds):
        row = move(r, d)
        for kind in kinds:
            @pl.when(p_cond(kind, row))
            def _(kind=kind):
                ref = place(kind, row)
                if kind >= DG:
                    pass_on(p_index(kind, row), ref, d, 2, kind - PS if kind > DG else None)
                else:
                    for order in range(2):
                        @pl.when(in_order(row, kind, order))
                        def _(order=order):
                            pass_on(p_index(kind, row), ref, d, order)

    def spread_tile(d, q):
        row = move(r, d)
        j = nth(q)

        @pl.when(j < tiles_of(row))
        def _():
            for order in range(2):
                @pl.when(in_order(row, j, order))
                def _(order=order):
                    pass_on(t_index(j, row), ftri.at[slot(row), j], d, order)

    def sent(k):
        total = 0
        for d in [0] + even:
            t = k ^ d

            def count(j):
                high = t >= R // 2 and not (t >= 3 * R // 4 and j % 2 == 1)
                return len(outs(d, int(high)))

            if t < KS:
                total += sum(count(n) for n in range(SPLIT)) + sum(count(j) for j in range(t))
            if t == KS % R:
                total += len(outs(d, 2))
        return total

    def drain():
        for k in range(R):
            if sent(k):
                @pl.when(r == k)
                def _(k=k):
                    whole, part = divmod(sent(k), KS)
                    for some in ([ftri.at[pl.ds(0, whole)]] if whole else []) + ([ftri.at[0, pl.ds(0, part)]] if part else []):
                        p_copy(0, some, 1).wait_send()
        for kind in psol + cols:
            for d in [0] + even:
                @pl.when(p_cond(kind, move(r, d)))
                def _(kind=kind, d=d):
                    for m in outs(d, 2):
                        p_copy(0, place(kind, KS % R), m, c_send.at[kind - PS, m // 2]).wait_send()

    def odd(row, kinds, tiles=False):
        @pl.when(lax.rem(r + row, 2) == 1)
        def _():
            for kind in kinds:
                when(p_cond(kind, row), lambda kind=kind: p_copy(p_index(kind, row), place(kind, row), 1).wait_recv())
            if tiles:
                def one(j, carry):
                    p_copy(t_index(j, row), ftri.at[slot(row), j], 1).wait_recv()
                    return carry

                lax.fori_loop(0, tiles_of(row), one, 0)

    near = [d for d in even if d & (d - 1) == 0]
    far = [d for d in even if d & (d - 1) != 0]
    bs = tuple(range(DG))
    psol = tuple(range(PS, CL))
    cols = tuple(range(CL, CL + CTD))

    loads[0].wait()
    z_start(DIA)

    @pl.when(z_cond(DIA, c))
    def _():
        diag[...] = pan_all[KS // R]
        spread(0, (DG,))

    loads[1].wait()
    loads[3].wait()
    for s in range(KF):
        @pl.when(z_cond(s, c))
        def _(s=s):
            ftri[slot(r), s * C + c] = dot(dtile[...], ftop[pl.ds(s, TILE, stride=KF), :])

        z_start(s)

    @pl.when(jnp.logical_and(k_own, c != dia_plane))
    def _():
        z_copy(DIA, 0, c).wait_recv()
        spread(0, (DG,))


    def scale_rhs():
        loads[2].wait()
        brow[mine] = dot(dtile[...], braw[...])

    when(b_own, scale_rhs)
    spread(0, bs)

    def own_tile(q, carry):
        j = nth(q)
        source = lax.rem(j, C)

        @pl.when(jnp.logical_and(j < tiles_of(r), source != c))
        def _():
            ref = ftri.at[slot(r), j]
            pltpu.make_async_remote_copy(
                src_ref=ref, dst_ref=ref, send_sem=z_send.at[0], recv_sem=z_recv.at[lax.div(j, C), source],
                device_id={"pcol": c}, device_id_type=MESH,
            ).wait_recv()

        spread_tile(0, q)
        return carry

    lax.fori_loop(0, KS, own_tile, 0)

    x_plane = jnp.where(c >= C // 2, C // 2 - 1, C // 2)
    x_slot = jnp.where(c >= C // 2, c - C // 2, C // 2 - 1 - c)

    def x_copy(k):
        return pltpu.make_async_remote_copy(
            src_ref=fbuf.at[pl.ds(I - EARLY, EARLY)], dst_ref=xbuf.at[k], send_sem=x_send.at[0], recv_sem=x_recv.at[k],
            device_id={"pcol": x_plane}, device_id_type=MESH,
        )

    loads[4].wait()
    if EARLY:
        x_copy(x_slot).start()
    n_pass(0)

    for d in even:
        spread(d, (DG,))
    odd(KS % R, (DG,))

    lanes = lax.broadcasted_iota(jnp.int32, (TILE, TILE), 1)
    rows = lax.broadcasted_iota(jnp.int32, (TILE, TILE), 0)
    tri[...] = diag[...]
    inv[...] = jnp.where(lanes == rows, 1.0, 0.0)

    lane = lanes[0:1]
    at_row = rows[:, 0:1]

    def pick(mask, values):
        return jnp.sum(jnp.where(mask, values, 0.0), axis=1, keepdims=True)

    def eliminate(b, carry):
        k = b * NB
        whole = tri[...]
        row = [tri[pl.ds(k + i, 1), :] for i in range(NB)]
        wrow = [inv[pl.ds(k + i, 1), :] for i in range(NB)]
        column = [pick(lanes == k + i, whole) for i in range(NB)]
        pivot = [[pick(lane == k + j, row[i]) if j >= i else None for j in range(NB)] for i in range(NB)]
        for i in range(NB):
            for h in range(i):
                factor_hi = pivot[h][i]
                for j in range(i, NB):
                    pivot[i][j] = pivot[i][j] - factor_hi * pivot[h][j]
                row[i] = row[i] - factor_hi * row[h]
                wrow[i] = wrow[i] - factor_hi * wrow[h]
                column[i] = column[i] - factor_hi * column[h]
            scale = 1.0 / jnp.sqrt(pivot[i][i])
            for j in range(i, NB):
                pivot[i][j] = pivot[i][j] * scale
            row[i] = jnp.where(lane >= k + i, row[i] * scale, 0.0)
            wrow[i] = wrow[i] * scale
            column[i] = column[i] * scale
        rest = inv[...]
        for i in range(NB):
            lcol = jnp.where(at_row > k + NB - 1, column[i], 0.0)
            whole = whole - lcol * row[i]
            rest = rest - lcol * wrow[i]
        tri[...] = whole
        inv[...] = rest
        for i in range(NB):
            tri[pl.ds(k + i, 1), :] = row[i]
            inv[pl.ds(k + i, 1), :] = wrow[i]
        return carry

    rounds = KS // 2 + 1
    count = 1 + 4 * rounds
    blocks = TILE // NB
    each = (blocks + count - 1) // count

    def part(n):
        lax.fori_loop(jnp.minimum(n * each, blocks), jnp.minimum((n + 1) * each, blocks), eliminate, 0)

    for d in near:
        spread(d, bs)
    part(0)
    for d in far:
        spread(d, bs)

    def relay(n, carry):
        for p in range(2):
            for d in near:
                @pl.when(n < rounds - 1)
                def _(d=d, p=p):
                    spread_tile(d, 2 * n + p)
            part(1 + 4 * n + p)
        for p in range(2):
            for d in far:
                @pl.when(n > 0)
                def _(d=d, p=p):
                    spread_tile(d, 2 * n - 2 + p)

            part(3 + 4 * n + p)
        return carry

    lax.fori_loop(0, rounds, relay, 0)
    inv_t[...] = inv[...].T
    n_pass(1)

    def arrived(t, carry):
        odd(t, bs)

        @pl.when(t > 0)
        def _():
            odd(t, (), True)

        return carry

    lax.fori_loop(0, KS, arrived, 0)
    for t in range(KS):
        total = brow[t]
        for j in range(t):
            total = total - dot(ftri[t, j], y[j], HIGH)
        y[t] = total


    def up_copy(n, src):
        return pltpu.make_async_remote_copy(
            src_ref=src.at[n], dst_ref=rin.at[n], send_sem=r_send.at[0], recv_sem=r_recv.at[n],
            device_id={"pcol": jnp.minimum(c + 1, C - 1)}, device_id_type=MESH,
        )

    def down_copy(n, src):
        return pltpu.make_async_remote_copy(
            src_ref=src.at[n], dst_ref=lin.at[n], send_sem=l_send.at[0], recv_sem=l_recv.at[n],
            device_id={"pcol": jnp.maximum(c - 1, 0)}, device_id_type=MESH,
        )

    def columns(tiles, plane):
        parts = [dot(tiles[pl.ds(s, TILE, stride=KF), :], y[s * C + plane], HIGH) for s in range(KF)]
        return sum(parts[1:], parts[0])

    def product(i):
        total = columns(fbuf.at[i], c)
        for h in range(SPLIT):
            n = (i - i0) * SPLIT + h
            own[n] = total[h * H:(h + 1) * H]

            @pl.when(c == 0)
            def _():
                up_copy(n, own).start()

            @pl.when(c == C - 1)
            def _():
                down_copy(n, own).start()

    for dist in range(2, C - 1):
        n_pass(dist)
    loads[5].wait()
    loads[6].wait()
    for i in range(i0):
        rbuf[i] = y[i * R + r]

    def strip_row(i):
        below = jnp.where(i * R + r > KS, dot(pan_all[i], inv_t[...], HIGH), 0.0)
        for s in range(CTD):
            at = pl.ds(s, TILE, stride=CTD)
            sbuf[i, at, :] = sbuf[i, at, :] - dot(below, colt[s], HIGH)
        rbuf[i] = rbuf[i] - dot(below, ps[...], HIGH)

    def total(n):
        return jnp.where(c == 0, lin[n], jnp.where(c == C - 1, rin[n], rin[n] + lin[n] - own[n]))

    def assemble(n, carry):
        i = i0 + lax.div(n, SPLIT)
        at = pl.ds(pl.multiple_of(lax.rem(n, SPLIT) * H, H), H)
        k = i * R + r
        rbuf[i, at, :] = rbuf[i, at, :] - total(n)

        @pl.when(k < KS)
        def _():
            rbuf[i, at, :] = y[slot(k), at, :]

        @pl.when(k == KS)
        def _():
            rbuf[i, at, :] = ps[at, :]

        return carry

    M = 4
    far_lag = (C - 1) * SKEW
    P0 = far_lag + SPLIT - 1
    S0 = P0 + 5
    ROWS = 2

    def rows_done(m):
        return jnp.clip(ROWS * (m - S0 + 1), 0, I - i0)

    def chunks_done(m):
        return jnp.clip(jnp.minimum(m - far_lag + 1, SPLIT * rows_done(m)), 0, N)

    def step(m, carry):
        nr = m - c * SKEW
        nl = m - (C - 1 - c) * SKEW

        @pl.when(m < I - i0)
        def _():
            product(m + i0)

        @pl.when(jnp.logical_and(c > 0, jnp.logical_and(nr >= 0, nr < jnp.where(c == C - 2, NS, N))))
        def _():
            up_copy(nr, rin).wait_recv()
            rin[nr] = rin[nr] + own[nr]

            @pl.when(jnp.logical_and(c < C - 1, nr < NS))
            def _():
                up_copy(nr, rin).start()

        @pl.when(jnp.logical_and(c < C - 1, jnp.logical_and(nl >= 0, nl < jnp.where(c == 1, NS, N))))
        def _():
            down_copy(nl, lin).wait_recv()
            lin[nl] = lin[nl] + own[nl]

            @pl.when(jnp.logical_and(c > 0, nl < NS))
            def _():
                down_copy(nl, lin).start()

        @pl.when(m == M)
        def _():
            n_pass(C - 1)
            for s in range(CTD):
                @pl.when(p_cond(CL + s, r))
                def _(s=s):
                    col[s] = pan_all[lax.div(wanted(s), R)]

            spread(0, cols)

        @pl.when(m == M + 2)
        def _():
            for d in even:
                spread(d, cols)

        @pl.when(m == M + 3)
        def _():
            for a in range(A):
                tile_a = (c * A + a) * R + r
                pbuf[a] = jnp.where(tile_a > KS, dot(pan_all[c * A + a], inv_t[...]), 0.0)

                @pl.when(tile_a == KS)
                def _(a=a):
                    pbuf[a] = tri[...].T

        @pl.when(m == M + 4)
        def _():
            for s in range(CTD):
                odd(lax.rem(wanted(s), R), (CL + s,))
            for s in range(CTD):
                colt[s] = dot(col[s], inv_t[...]).T

        @pl.when(jnp.logical_and(m == P0, k_own))
        def _():
            for h in range(SPLIT):
                rest[pl.ds(h * H, H), :] = rbuf[i0, pl.ds(h * H, H), :] - total(h)
            ps[...] = dot(inv[...], rest[...])
            spread(0, psol)

        @pl.when(m == P0 + 3)
        def _():
            for d in even:
                spread(d, psol)

        @pl.when(m == P0 + 4)
        def _():
            odd(KS % R, psol)

        def one_row(n, carry):
            strip_row(n + i0)
            return carry

        lax.fori_loop(rows_done(m - 1), rows_done(m), one_row, 0)
        lax.fori_loop(chunks_done(m - 1), chunks_done(m), assemble, 0)
        return carry

    def whole_sum(e, carry):
        i = I - EARLY + e
        mine = columns(fbuf.at[i], c)
        whole = mine
        for k in range(2):
            whole = whole + columns(xbuf.at[k, e], jnp.where(c >= C // 2, C // 2 - 1 - k, C // 2 + k))
        for h in range(SPLIT):
            n = NS + e * SPLIT + h

            @pl.when(c < C // 2)
            def _():
                lin[n] = whole[h * H:(h + 1) * H]
                down_copy(n, lin).start()

            @pl.when(c >= C // 2)
            def _():
                rin[n] = whole[h * H:(h + 1) * H]
                up_copy(n, rin).start()

        return carry

    if EARLY:
        @pl.when(jnp.logical_and(c > 0, c < C - 1))
        def _():
            for k in range(2):
                x_copy(k).wait_recv()
            lax.fori_loop(0, EARLY, whole_sum, 0)

    lax.fori_loop(0, N + far_lag, step, 0)

    for kind in range(KF):
        z_wait_send(kind)
    z_wait_send(DIA)
    n_done()
    drain()

    if EARLY:
        x_copy(0).wait_send()

    def all_sent(buf, sem, count):
        some = buf.at[pl.ds(0, count)]
        pltpu.make_async_remote_copy(
            src_ref=some, dst_ref=some, send_sem=sem.at[0], recv_sem=x_recv.at[0],
            device_id={"pcol": c}, device_id_type=MESH,
        ).wait_send()

    fewer = EARLY > 0
    for bound, short, buf, sem in ((c < C - 1, C // 2 - 1, rin, r_send), (c > 0, C // 2, lin, l_send)):
        @pl.when(jnp.logical_and(bound, c != short) if fewer else bound)
        def _(buf=buf, sem=sem):
            all_sent(buf, sem, N)

        if fewer:
            @pl.when(c == short)
            def _(buf=buf, sem=sem):
                all_sent(buf, sem, NS)


def per_device(panel, strip, factor, inv_diag, rhs):
    R = lax.axis_size("prow")
    C = lax.axis_size("pcol")
    A, TILE, _ = panel.shape
    I, _, CTD, _ = strip.shape
    KF = factor.shape[2]
    NR = rhs.shape[2]
    KS = KF * C
    assert KS <= R and R & (R - 1) == 0 and KS % 2 == 0 and NR == SPLIT * TILE
    f32 = jnp.float32
    N = (I - KS // R) * SPLIT
    H = TILE // SPLIT
    early = EARLY_TILES if C == 4 else 0
    dma = pltpu.SemaphoreType.DMA
    shapes = (panel.shape, (I, TILE * CTD, TILE), rhs.shape)
    done = pl.pallas_call(
        functools.partial(kernel, R, C, CTD, KF),
        out_shape=[pltpu.VMEM(shape, f32) for shape in shapes],
        in_specs=[pl.BlockSpec(memory_space=pltpu.HBM)] * 5,
        out_specs=[pl.BlockSpec(memory_space=pltpu.VMEM)] * 3,
        scratch_shapes=[
            pltpu.VMEM((I, TILE, TILE), f32),
            pltpu.VMEM((TILE, TILE), f32),
            pltpu.VMEM((CTD, TILE, TILE), f32),
            pltpu.VMEM((CTD, TILE, TILE), f32),
            pltpu.VMEM((TILE * KF, TILE), f32),
            pltpu.VMEM((TILE, NR), f32),
            pltpu.VMEM((TILE, TILE), f32),
            pltpu.VMEM((KS, KS, TILE, TILE), f32),
            pltpu.VMEM((KS, TILE, NR), f32),
            pltpu.VMEM((KS, TILE, NR), f32),
            pltpu.VMEM((I, TILE * KF, TILE), f32),
            pltpu.VMEM((2, early, TILE * KF, TILE), f32),
            pltpu.VMEM((N, H, NR), f32),
            pltpu.VMEM((N, H, NR), f32),
            pltpu.VMEM((N, H, NR), f32),
            pltpu.VMEM((TILE, TILE), f32),
            pltpu.VMEM((TILE, TILE), f32),
            pltpu.VMEM((TILE, TILE), f32),
            pltpu.VMEM((TILE, NR), f32),
            pltpu.VMEM((TILE, NR), f32),
            dma((KF + 1,)),
            dma((KF + 1, C)),
            dma((2, C)),
            dma((C,)),
            dma((1,)),
            dma((KS * SPLIT + 1 + SPLIT + CTD + KS * (KS - 1) // 2,)),
            dma((SPLIT + CTD, R // 2)),
            dma((1,)),
            dma((2,)),
            dma((1,)),
            dma((N,)),
            dma((1,)),
            dma((N,)),
            dma((7,)),
        ],
        compiler_params=pltpu.CompilerParams(
            collective_id=0, has_side_effects=True, vmem_limit_bytes=44 << 20
        ),
    )(
        *(
            pltpu.with_memory_space_constraint(one, pltpu.HBM)
            for one in (
                panel,
                strip.reshape(I, TILE * CTD, TILE),
                factor.reshape(I, TILE * KF, TILE),
                inv_diag,
                rhs,
            )
        )
    )
    panel_factor, new_strip, forward = pl.pallas_call(
        copies,
        out_shape=[jax.ShapeDtypeStruct(shape, f32) for shape in shapes],
        in_specs=[pl.BlockSpec(memory_space=pltpu.VMEM)] * 3,
        out_specs=[pl.BlockSpec(memory_space=pl.ANY)] * 3,
        scratch_shapes=[dma((3,))],
        compiler_params=pltpu.CompilerParams(vmem_limit_bytes=16 << 20),
    )(*done)
    return panel_factor, new_strip.reshape(strip.shape), forward


def solution(mesh):
    in_specs = (
        P("pcol", "prow", None),
        P(None, "prow", None, "pcol"),
        P(None, "prow", None, "pcol"),
        P(),
        P(None, "prow", None),
    )
    out_specs = (P("pcol", "prow", None), P(None, "prow", None, "pcol"), P(None, "prow", None))
    return jax.shard_map(
        per_device, mesh=mesh, in_specs=in_specs, out_specs=out_specs, check_vma=False
    )
```

```python
import functools

import jax
import jax.numpy as jnp
from jax import lax
from jax.experimental import pallas as pl
from jax.experimental.pallas import tpu as pltpu
from jax.sharding import PartitionSpec as P

HIGHEST = lax.Precision.HIGHEST
HIGH = lax.Precision.HIGH
MESH = pl.DeviceIdType.MESH
SPLIT = 2
EARLY_TILES = 1
SKEW = 3
NB = 4


def dot(a, b, precision=HIGHEST):
    return jnp.dot(a, b, precision=precision, preferred_element_type=jnp.float32)


def when(cond, body):
    if cond is True:
        body()
    elif cond is not False:
        pl.when(cond)(body)


def flip(v, m):
    return v + m - 2 * m * lax.rem(lax.div(v, m), 2)


def copies(panel, strip, forward, panel_out, strip_out, forward_out, sem):
    pairs = ((forward, forward_out), (strip, strip_out), (panel, panel_out))
    made = [pltpu.make_async_copy(src, dst, sem.at[n]) for n, (src, dst) in enumerate(pairs)]
    for one in made:
        one.start()
    for one in made:
        one.wait()


def kernel(
    R, C, CTD, KF,
    panel, strip, factor, inv_diag, rhs,
    pbuf, sbuf, rbuf,
    pan_all, diag, col, colt, ftop, braw, dtile, ftri, brow, y, fbuf, xbuf, own, rin, lin, tri, inv, inv_t, ps, rest,
    z_send, z_recv, n_send, n_recv, p_send, p_recv, c_send, x_send, x_recv, r_send, r_recv, l_send, l_recv, in_sem,
):
    r = lax.axis_index("prow")
    c = lax.axis_index("pcol")
    A, TILE, _ = panel.shape
    I = factor.shape[0]
    KS = KF * C
    full = KS == R
    i0 = KS // R
    H = TILE // SPLIT
    N = (I - i0) * SPLIT
    EARLY = xbuf.shape[1]
    NS = N - EARLY * SPLIT

    def slot(row):
        return jnp.minimum(row, KS - 1)

    def tiles_of(row):
        return jnp.where(row < KS, row, 0)

    b_own = True if full else r < KS
    k_own = r == KS % R
    mine = jnp.minimum(r, KS - 1)

    def load(n, src, dst):
        return pltpu.make_async_copy(src, dst, in_sem.at[n])

    loads = [
        load(0, panel, pan_all.at[pl.ds(c * A, A)]),
        load(1, factor.at[0], ftop),
        load(2, rhs.at[0], braw),
        load(3, inv_diag.at[mine], dtile),
        load(4, factor, fbuf),
        load(5, rhs, rbuf),
        load(6, strip, sbuf),
    ]
    conds = [True, True, b_own, True, True, True, True]
    for cond, one in zip(conds, loads):
        when(cond, one.start)

    dims = []
    m = 2
    while m < R:
        dims.append(m)
        m *= 2
    seqs = (dims + [1], dims[::-1] + [1])
    even = list(range(2, R, 2))

    def move(v, d):
        for m in seqs[0]:
            if d & m:
                v = flip(v, m)
        return v

    barrier = pltpu.get_barrier_semaphore()

    @pl.loop(1, C)
    def _(d):
        pl.semaphore_signal(barrier, inc=1, device_id={"pcol": lax.rem(c + d, C)}, device_id_type=MESH)

    for d in even + [1]:
        pl.semaphore_signal(barrier, inc=1, device_id={"prow": move(r, d)}, device_id_type=MESH)
    pl.semaphore_wait(barrier, C - 1 + len(even) + 1)

    DIA = KF
    dia_plane = KS // R // A

    def z_copy(kind, source, place):
        if kind is DIA:
            src, dst, at = pan_all.at[KS // R], diag, (KF, 0)
        else:
            src = dst = ftri.at[slot(r), kind * C + source]
            at = (kind, source)
        return pltpu.make_async_remote_copy(
            src_ref=src, dst_ref=dst, send_sem=z_send.at[at[0]], recv_sem=z_recv.at[at],
            device_id={"pcol": place}, device_id_type=MESH,
        )

    def z_cond(kind, source):
        if kind is DIA:
            return jnp.logical_and(k_own, source == dia_plane)
        return kind * C + source < tiles_of(r)

    def z_start(kind):
        @pl.when(z_cond(kind, c))
        def _():
            for d in range(1, C):
                z_copy(kind, c, lax.rem(c + d, C)).start()

    def z_wait_send(kind):
        @pl.when(z_cond(kind, c))
        def _():
            some = ftri.at[0, pl.ds(0, C - 1)]
            pltpu.make_async_remote_copy(
                src_ref=some, dst_ref=some, send_sem=z_send.at[kind], recv_sem=z_recv.at[0, 0],
                device_id={"pcol": c}, device_id_type=MESH,
            ).wait_send()

    def n_copy(source, way):
        ref = pan_all.at[pl.ds(source * A, A)]
        return pltpu.make_async_remote_copy(
            src_ref=ref, dst_ref=ref, send_sem=n_send.at[way, source], recv_sem=n_recv.at[source],
            device_id={"pcol": jnp.clip(c + (1 if way else -1), 0, C - 1)}, device_id_type=MESH,
        )

    def n_pass(dist):
        for way in (1, 0):
            source = c - dist if way else c + dist
            has = source >= 0 if way else source < C
            more = c < C - 1 if way else c > 0

            @pl.when(has)
            def _(way=way, source=source, more=more):
                if dist:
                    n_copy(source, way).wait_recv()

                @pl.when(more)
                def _():
                    n_copy(source, way).start()

    def n_done():
        @pl.loop(0, C)
        def _(source):
            @pl.when(jnp.logical_and(source <= c, c < C - 1))
            def _():
                n_copy(source, 1).wait_send()

            @pl.when(jnp.logical_and(source >= c, c > 0))
            def _():
                n_copy(source, 0).wait_send()

    DG, PS, CL = SPLIT, SPLIT + 1, 2 * SPLIT + 1

    def wanted(s):
        return KS + 1 + s * C + c

    def place(kind, row):
        if kind < DG:
            return brow.at[slot(row), pl.ds(kind * H, H)]
        if kind == DG:
            return diag
        if kind < CL:
            return ps.at[pl.ds((kind - PS) * H, H)]
        return col.at[kind - CL]

    T0 = KS * SPLIT + 1 + SPLIT + CTD

    def p_index(kind, row):
        if kind < DG:
            return slot(row) * SPLIT + kind
        return KS * SPLIT + kind - DG

    def t_index(j, row):
        return T0 + lax.div(row * (row - 1), 2) + j

    def p_cond(kind, row):
        if kind < DG:
            return True if full else row < KS
        if kind < CL:
            return row == KS % R
        return row == lax.rem(wanted(kind - CL), R)

    def in_order(row, j, order):
        last = row >= 3 * R // 4
        odd_one = lax.rem(j, 2) == 1
        high = jnp.logical_and(row >= R // 2, jnp.logical_not(jnp.logical_and(last, odd_one)))
        return high if order else jnp.logical_not(high)

    def nth(q):
        k = lax.div(q, KF)
        away = jnp.where(lax.rem(k, 2) == 1, lax.div(k + 1, 2), C - lax.div(k, 2))
        return lax.rem(q, KF) * C + lax.rem(c + away, C)

    def p_copy(index, ref, d, sem=None):
        return pltpu.make_async_remote_copy(
            src_ref=ref, dst_ref=ref, send_sem=p_send.at[0] if sem is None else sem, recv_sem=p_recv.at[index],
            device_id={"prow": move(r, d)}, device_id_type=MESH,
        )

    def outs(d, order):
        if order == 2:
            return [1] if d else even + [1]
        seq = seqs[order]
        at = max([n for n, m in enumerate(seq) if d & m], default=-1)
        return seq[at + 1:]

    def pass_on(index, ref, d, order, s=None):
        if d:
            p_copy(index, ref, 1).wait_recv()
        for m in outs(d, order):
            p_copy(index, ref, m, None if s is None else c_send.at[s, m // 2]).start()

    def spread(d, kinds):
        row = move(r, d)
        for kind in kinds:
            @pl.when(p_cond(kind, row))
            def _(kind=kind):
                ref = place(kind, row)
                if kind >= DG:
                    pass_on(p_index(kind, row), ref, d, 2, kind - PS if kind > DG else None)
                else:
                    for order in range(2):
                        @pl.when(in_order(row, kind, order))
                        def _(order=order):
                            pass_on(p_index(kind, row), ref, d, order)

    def spread_tile(d, q):
        row = move(r, d)
        j = nth(q)

        @pl.when(j < tiles_of(row))
        def _():
            for order in range(2):
                @pl.when(in_order(row, j, order))
                def _(order=order):
                    pass_on(t_index(j, row), ftri.at[slot(row), j], d, order)

    def sent(k):
        total = 0
        for d in [0] + even:
            t = k ^ d

            def count(j):
                high = t >= R // 2 and not (t >= 3 * R // 4 and j % 2 == 1)
                return len(outs(d, int(high)))

            if t < KS:
                total += sum(count(n) for n in range(SPLIT)) + sum(count(j) for j in range(t))
            if t == KS % R:
                total += len(outs(d, 2))
        return total

    def drain():
        for k in range(R):
            if sent(k):
                @pl.when(r == k)
                def _(k=k):
                    whole, part = divmod(sent(k), KS)
                    for some in ([ftri.at[pl.ds(0, whole)]] if whole else []) + ([ftri.at[0, pl.ds(0, part)]] if part else []):
                        p_copy(0, some, 1).wait_send()
        for kind in psol + cols:
            for d in [0] + even:
                @pl.when(p_cond(kind, move(r, d)))
                def _(kind=kind, d=d):
                    for m in outs(d, 2):
                        p_copy(0, place(kind, KS % R), m, c_send.at[kind - PS, m // 2]).wait_send()

    def odd(row, kinds, tiles=False):
        @pl.when(lax.rem(r + row, 2) == 1)
        def _():
            for kind in kinds:
                when(p_cond(kind, row), lambda kind=kind: p_copy(p_index(kind, row), place(kind, row), 1).wait_recv())
            if tiles:
                def one(j, carry):
                    p_copy(t_index(j, row), ftri.at[slot(row), j], 1).wait_recv()
                    return carry

                lax.fori_loop(0, tiles_of(row), one, 0)

    near = [d for d in even if d & (d - 1) == 0]
    far = [d for d in even if d & (d - 1) != 0]
    bs = tuple(range(DG))
    psol = tuple(range(PS, CL))
    cols = tuple(range(CL, CL + CTD))

    loads[0].wait()
    z_start(DIA)

    @pl.when(z_cond(DIA, c))
    def _():
        diag[...] = pan_all[KS // R]
        spread(0, (DG,))

    loads[1].wait()
    loads[3].wait()
    for s in range(KF):
        @pl.when(z_cond(s, c))
        def _(s=s):
            ftri[slot(r), s * C + c] = dot(dtile[...], ftop[pl.ds(s, TILE, stride=KF), :])

        z_start(s)

    @pl.when(jnp.logical_and(k_own, c != dia_plane))
    def _():
        z_copy(DIA, 0, c).wait_recv()
        spread(0, (DG,))


    def scale_rhs():
        loads[2].wait()
        brow[mine] = dot(dtile[...], braw[...])

    when(b_own, scale_rhs)
    spread(0, bs)

    def own_tile(q, carry):
        j = nth(q)
        source = lax.rem(j, C)

        @pl.when(jnp.logical_and(j < tiles_of(r), source != c))
        def _():
            ref = ftri.at[slot(r), j]
            pltpu.make_async_remote_copy(
                src_ref=ref, dst_ref=ref, send_sem=z_send.at[0], recv_sem=z_recv.at[lax.div(j, C), source],
                device_id={"pcol": c}, device_id_type=MESH,
            ).wait_recv()

        spread_tile(0, q)
        return carry

    n_pass(0)
    lax.fori_loop(0, KS, own_tile, 0)

    x_plane = jnp.where(c >= C // 2, C // 2 - 1, C // 2)
    x_slot = jnp.where(c >= C // 2, c - C // 2, C // 2 - 1 - c)

    def x_copy(k):
        return pltpu.make_async_remote_copy(
            src_ref=fbuf.at[pl.ds(I - EARLY, EARLY)], dst_ref=xbuf.at[k], send_sem=x_send.at[0], recv_sem=x_recv.at[k],
            device_id={"pcol": x_plane}, device_id_type=MESH,
        )

    loads[4].wait()
    if EARLY:
        x_copy(x_slot).start()

    for d in even:
        spread(d, (DG,))
    odd(KS % R, (DG,))

    lanes = lax.broadcasted_iota(jnp.int32, (TILE, TILE), 1)
    rows = lax.broadcasted_iota(jnp.int32, (TILE, TILE), 0)
    tri[...] = diag[...]
    inv[...] = jnp.where(lanes == rows, 1.0, 0.0)

    lane = lanes[0:1]
    at_row = rows[:, 0:1]

    def pick(mask, values):
        return jnp.sum(jnp.where(mask, values, 0.0), axis=1, keepdims=True)

    def eliminate(b, carry):
        k = b * NB
        whole = tri[...]
        row = [tri[pl.ds(k + i, 1), :] for i in range(NB)]
        wrow = [inv[pl.ds(k + i, 1), :] for i in range(NB)]
        column = [pick(lanes == k + i, whole) for i in range(NB)]
        pivot = [[pick(lane == k + j, row[i]) if j >= i else None for j in range(NB)] for i in range(NB)]
        for i in range(NB):
            for h in range(i):
                factor_hi = pivot[h][i]
                for j in range(i, NB):
                    pivot[i][j] = pivot[i][j] - factor_hi * pivot[h][j]
                row[i] = row[i] - factor_hi * row[h]
                wrow[i] = wrow[i] - factor_hi * wrow[h]
                column[i] = column[i] - factor_hi * column[h]
            scale = 1.0 / jnp.sqrt(pivot[i][i])
            for j in range(i, NB):
                pivot[i][j] = pivot[i][j] * scale
            row[i] = jnp.where(lane >= k + i, row[i] * scale, 0.0)
            wrow[i] = wrow[i] * scale
            column[i] = column[i] * scale
        rest = inv[...]
        for i in range(NB):
            lcol = jnp.where(at_row > k + NB - 1, column[i], 0.0)
            whole = whole - lcol * row[i]
            rest = rest - lcol * wrow[i]
        tri[...] = whole
        inv[...] = rest
        for i in range(NB):
            tri[pl.ds(k + i, 1), :] = row[i]
            inv[pl.ds(k + i, 1), :] = wrow[i]
        return carry

    rounds = KS // 2 + 1
    count = 1 + 4 * rounds
    blocks = TILE // NB
    each = (blocks + count - 1) // count

    def part(n):
        lax.fori_loop(jnp.minimum(n * each, blocks), jnp.minimum((n + 1) * each, blocks), eliminate, 0)

    for d in near:
        spread(d, bs)
    part(0)
    for d in far:
        spread(d, bs)

    def relay(n, carry):
        for p in range(2):
            for d in near:
                @pl.when(n < rounds - 1)
                def _(d=d, p=p):
                    spread_tile(d, 2 * n + p)
            part(1 + 4 * n + p)
        for p in range(2):
            for d in far:
                @pl.when(n > 0)
                def _(d=d, p=p):
                    spread_tile(d, 2 * n - 2 + p)

            part(3 + 4 * n + p)
        return carry

    n_pass(1)
    lax.fori_loop(0, rounds, relay, 0)
    for dist in range(2, C - 1):
        n_pass(dist)
    inv_t[...] = inv[...].T

    def arrived(t, carry):
        odd(t, bs)

        @pl.when(t > 0)
        def _():
            odd(t, (), True)

        return carry

    lax.fori_loop(0, KS, arrived, 0)
    for t in range(KS):
        total = brow[t]
        for j in range(t):
            total = total - dot(ftri[t, j], y[j], HIGH)
        y[t] = total


    def up_copy(n, src):
        return pltpu.make_async_remote_copy(
            src_ref=src.at[n], dst_ref=rin.at[n], send_sem=r_send.at[0], recv_sem=r_recv.at[n],
            device_id={"pcol": jnp.minimum(c + 1, C - 1)}, device_id_type=MESH,
        )

    def down_copy(n, src):
        return pltpu.make_async_remote_copy(
            src_ref=src.at[n], dst_ref=lin.at[n], send_sem=l_send.at[0], recv_sem=l_recv.at[n],
            device_id={"pcol": jnp.maximum(c - 1, 0)}, device_id_type=MESH,
        )

    def columns(tiles, plane):
        parts = [dot(tiles[pl.ds(s, TILE, stride=KF), :], y[s * C + plane], HIGH) for s in range(KF)]
        return sum(parts[1:], parts[0])

    def product(i):
        total = columns(fbuf.at[i], c)
        for h in range(SPLIT):
            n = (i - i0) * SPLIT + h
            own[n] = total[h * H:(h + 1) * H]

            @pl.when(c == 0)
            def _():
                up_copy(n, own).start()

            @pl.when(c == C - 1)
            def _():
                down_copy(n, own).start()

    loads[5].wait()
    loads[6].wait()
    for i in range(i0):
        rbuf[i] = y[i * R + r]

    def strip_row(i):
        below = jnp.where(i * R + r > KS, dot(pan_all[i], inv_t[...], HIGH), 0.0)
        for s in range(CTD):
            at = pl.ds(s, TILE, stride=CTD)
            sbuf[i, at, :] = sbuf[i, at, :] - dot(below, colt[s], HIGH)
        rbuf[i] = rbuf[i] - dot(below, ps[...], HIGH)

    def total(n):
        return jnp.where(c == 0, lin[n], jnp.where(c == C - 1, rin[n], rin[n] + lin[n] - own[n]))

    def assemble(n, carry):
        i = i0 + lax.div(n, SPLIT)
        at = pl.ds(pl.multiple_of(lax.rem(n, SPLIT) * H, H), H)
        k = i * R + r
        rbuf[i, at, :] = rbuf[i, at, :] - total(n)

        @pl.when(k < KS)
        def _():
            rbuf[i, at, :] = y[slot(k), at, :]

        @pl.when(k == KS)
        def _():
            rbuf[i, at, :] = ps[at, :]

        return carry

    M = 4
    far_lag = (C - 1) * SKEW
    P0 = far_lag + SPLIT - 1
    S0 = P0 + 5
    ROWS = 2

    def rows_done(m):
        return jnp.clip(ROWS * (m - S0 + 1), 0, I - i0)

    def chunks_done(m):
        return jnp.clip(jnp.minimum(m - far_lag + 1, SPLIT * rows_done(m)), 0, N)

    def step(m, carry):
        nr = m - c * SKEW
        nl = m - (C - 1 - c) * SKEW

        @pl.when(m < I - i0)
        def _():
            product(m + i0)

        @pl.when(jnp.logical_and(c > 0, jnp.logical_and(nr >= 0, nr < jnp.where(c == C - 2, NS, N))))
        def _():
            up_copy(nr, rin).wait_recv()
            rin[nr] = rin[nr] + own[nr]

            @pl.when(jnp.logical_and(c < C - 1, nr < NS))
            def _():
                up_copy(nr, rin).start()

        @pl.when(jnp.logical_and(c < C - 1, jnp.logical_and(nl >= 0, nl < jnp.where(c == 1, NS, N))))
        def _():
            down_copy(nl, lin).wait_recv()
            lin[nl] = lin[nl] + own[nl]

            @pl.when(jnp.logical_and(c > 0, nl < NS))
            def _():
                down_copy(nl, lin).start()

        @pl.when(m == M)
        def _():
            n_pass(C - 1)
            for s in range(CTD):
                @pl.when(p_cond(CL + s, r))
                def _(s=s):
                    col[s] = pan_all[lax.div(wanted(s), R)]

            spread(0, cols)

        @pl.when(m == M + 2)
        def _():
            for d in even:
                spread(d, cols)

        @pl.when(m == M + 3)
        def _():
            for a in range(A):
                tile_a = (c * A + a) * R + r
                pbuf[a] = jnp.where(tile_a > KS, dot(pan_all[c * A + a], inv_t[...]), 0.0)

                @pl.when(tile_a == KS)
                def _(a=a):
                    pbuf[a] = tri[...].T

        @pl.when(m == M + 4)
        def _():
            for s in range(CTD):
                odd(lax.rem(wanted(s), R), (CL + s,))
            for s in range(CTD):
                colt[s] = dot(col[s], inv_t[...]).T

        @pl.when(jnp.logical_and(m == P0, k_own))
        def _():
            for h in range(SPLIT):
                rest[pl.ds(h * H, H), :] = rbuf[i0, pl.ds(h * H, H), :] - total(h)
            ps[...] = dot(inv[...], rest[...])
            spread(0, psol)

        @pl.when(m == P0 + 3)
        def _():
            for d in even:
                spread(d, psol)

        @pl.when(m == P0 + 4)
        def _():
            odd(KS % R, psol)

        def one_row(n, carry):
            strip_row(n + i0)
            return carry

        lax.fori_loop(rows_done(m - 1), rows_done(m), one_row, 0)
        lax.fori_loop(chunks_done(m - 1), chunks_done(m), assemble, 0)
        return carry

    def whole_sum(e, carry):
        i = I - EARLY + e
        mine = columns(fbuf.at[i], c)
        whole = mine
        for k in range(2):
            whole = whole + columns(xbuf.at[k, e], jnp.where(c >= C // 2, C // 2 - 1 - k, C // 2 + k))
        for h in range(SPLIT):
            n = NS + e * SPLIT + h

            @pl.when(c < C // 2)
            def _():
                lin[n] = whole[h * H:(h + 1) * H]
                down_copy(n, lin).start()

            @pl.when(c >= C // 2)
            def _():
                rin[n] = whole[h * H:(h + 1) * H]
                up_copy(n, rin).start()

        return carry

    if EARLY:
        @pl.when(jnp.logical_and(c > 0, c < C - 1))
        def _():
            for k in range(2):
                x_copy(k).wait_recv()
            lax.fori_loop(0, EARLY, whole_sum, 0)

    lax.fori_loop(0, N + far_lag, step, 0)

    for kind in range(KF):
        z_wait_send(kind)
    z_wait_send(DIA)
    n_done()
    drain()

    if EARLY:
        x_copy(0).wait_send()

    def all_sent(buf, sem, count):
        some = buf.at[pl.ds(0, count)]
        pltpu.make_async_remote_copy(
            src_ref=some, dst_ref=some, send_sem=sem.at[0], recv_sem=x_recv.at[0],
            device_id={"pcol": c}, device_id_type=MESH,
        ).wait_send()

    fewer = EARLY > 0
    for bound, short, buf, sem in ((c < C - 1, C // 2 - 1, rin, r_send), (c > 0, C // 2, lin, l_send)):
        @pl.when(jnp.logical_and(bound, c != short) if fewer else bound)
        def _(buf=buf, sem=sem):
            all_sent(buf, sem, N)

        if fewer:
            @pl.when(c == short)
            def _(buf=buf, sem=sem):
                all_sent(buf, sem, NS)


def per_device(panel, strip, factor, inv_diag, rhs):
    R = lax.axis_size("prow")
    C = lax.axis_size("pcol")
    A, TILE, _ = panel.shape
    I, _, CTD, _ = strip.shape
    KF = factor.shape[2]
    NR = rhs.shape[2]
    KS = KF * C
    assert KS <= R and R & (R - 1) == 0 and KS % 2 == 0 and NR == SPLIT * TILE
    f32 = jnp.float32
    N = (I - KS // R) * SPLIT
    H = TILE // SPLIT
    early = EARLY_TILES if C == 4 else 0
    dma = pltpu.SemaphoreType.DMA
    shapes = (panel.shape, (I, TILE * CTD, TILE), rhs.shape)
    done = pl.pallas_call(
        functools.partial(kernel, R, C, CTD, KF),
        out_shape=[pltpu.VMEM(shape, f32) for shape in shapes],
        in_specs=[pl.BlockSpec(memory_space=pltpu.HBM)] * 5,
        out_specs=[pl.BlockSpec(memory_space=pltpu.VMEM)] * 3,
        scratch_shapes=[
            pltpu.VMEM((I, TILE, TILE), f32),
            pltpu.VMEM((TILE, TILE), f32),
            pltpu.VMEM((CTD, TILE, TILE), f32),
            pltpu.VMEM((CTD, TILE, TILE), f32),
            pltpu.VMEM((TILE * KF, TILE), f32),
            pltpu.VMEM((TILE, NR), f32),
            pltpu.VMEM((TILE, TILE), f32),
            pltpu.VMEM((KS, KS, TILE, TILE), f32),
            pltpu.VMEM((KS, TILE, NR), f32),
            pltpu.VMEM((KS, TILE, NR), f32),
            pltpu.VMEM((I, TILE * KF, TILE), f32),
            pltpu.VMEM((2, early, TILE * KF, TILE), f32),
            pltpu.VMEM((N, H, NR), f32),
            pltpu.VMEM((N, H, NR), f32),
            pltpu.VMEM((N, H, NR), f32),
            pltpu.VMEM((TILE, TILE), f32),
            pltpu.VMEM((TILE, TILE), f32),
            pltpu.VMEM((TILE, TILE), f32),
            pltpu.VMEM((TILE, NR), f32),
            pltpu.VMEM((TILE, NR), f32),
            dma((KF + 1,)),
            dma((KF + 1, C)),
            dma((2, C)),
            dma((C,)),
            dma((1,)),
            dma((KS * SPLIT + 1 + SPLIT + CTD + KS * (KS - 1) // 2,)),
            dma((SPLIT + CTD, R // 2)),
            dma((1,)),
            dma((2,)),
            dma((1,)),
            dma((N,)),
            dma((1,)),
            dma((N,)),
            dma((7,)),
        ],
        compiler_params=pltpu.CompilerParams(
            collective_id=0, has_side_effects=True, vmem_limit_bytes=44 << 20
        ),
    )(
        *(
            pltpu.with_memory_space_constraint(one, pltpu.HBM)
            for one in (
                panel,
                strip.reshape(I, TILE * CTD, TILE),
                factor.reshape(I, TILE * KF, TILE),
                inv_diag,
                rhs,
            )
        )
    )
    panel_factor, new_strip, forward = pl.pallas_call(
        copies,
        out_shape=[jax.ShapeDtypeStruct(shape, f32) for shape in shapes],
        in_specs=[pl.BlockSpec(memory_space=pltpu.VMEM)] * 3,
        out_specs=[pl.BlockSpec(memory_space=pl.ANY)] * 3,
        scratch_shapes=[dma((3,))],
        compiler_params=pltpu.CompilerParams(vmem_limit_bytes=16 << 20),
    )(*done)
    return panel_factor, new_strip.reshape(strip.shape), forward


def solution(mesh):
    in_specs = (
        P("pcol", "prow", None),
        P(None, "prow", None, "pcol"),
        P(None, "prow", None, "pcol"),
        P(),
        P(None, "prow", None),
    )
    out_specs = (P("pcol", "prow", None), P(None, "prow", None, "pcol"), P(None, "prow", None))
    return jax.shard_map(
        per_device, mesh=mesh, in_specs=in_specs, out_specs=out_specs, check_vma=False
    )
```

```python
import functools

import jax
import jax.numpy as jnp
from jax import lax
from jax.experimental import pallas as pl
from jax.experimental.pallas import tpu as pltpu
from jax.sharding import PartitionSpec as P

HIGHEST = lax.Precision.HIGHEST
HIGH = lax.Precision.HIGH
MESH = pl.DeviceIdType.MESH
SPLIT = 2
EARLY_TILES = 1
SKEW = 3
NB = 4


def dot(a, b, precision=HIGHEST):
    return jnp.dot(a, b, precision=precision, preferred_element_type=jnp.float32)


def when(cond, body):
    if cond is True:
        body()
    elif cond is not False:
        pl.when(cond)(body)


def flip(v, m):
    return v + m - 2 * m * lax.rem(lax.div(v, m), 2)


def copies(panel, strip, forward, panel_out, strip_out, forward_out, sem):
    pairs = ((forward, forward_out), (strip, strip_out), (panel, panel_out))
    made = [pltpu.make_async_copy(src, dst, sem.at[n]) for n, (src, dst) in enumerate(pairs)]
    for one in made:
        one.start()
    for one in made:
        one.wait()


def kernel(
    R, C, CTD, KF,
    panel, strip, factor, inv_diag, rhs,
    pbuf, sbuf, rbuf,
    pan_all, diag, col, colt, ftop, braw, dtile, ftri, brow, y, fbuf, xbuf, own, rin, lin, tri, inv, inv_t, ps, rest,
    z_send, z_recv, n_send, n_recv, p_send, p_recv, c_send, x_send, x_recv, r_send, r_recv, l_send, l_recv, in_sem,
):
    r = lax.axis_index("prow")
    c = lax.axis_index("pcol")
    A, TILE, _ = panel.shape
    I = factor.shape[0]
    KS = KF * C
    full = KS == R
    i0 = KS // R
    H = TILE // SPLIT
    N = (I - i0) * SPLIT
    EARLY = xbuf.shape[1]
    NS = N - EARLY * SPLIT

    def slot(row):
        return jnp.minimum(row, KS - 1)

    def tiles_of(row):
        return jnp.where(row < KS, row, 0)

    b_own = True if full else r < KS
    k_own = r == KS % R
    mine = jnp.minimum(r, KS - 1)

    def load(n, src, dst):
        return pltpu.make_async_copy(src, dst, in_sem.at[n])

    loads = [
        load(0, panel, pan_all.at[pl.ds(c * A, A)]),
        load(1, factor.at[0], ftop),
        load(2, rhs.at[0], braw),
        load(3, inv_diag.at[mine], dtile),
        load(4, factor, fbuf),
        load(5, rhs, rbuf),
        load(6, strip, sbuf),
    ]
    conds = [True, True, b_own, True, True, True, True]
    for cond, one in zip(conds, loads):
        when(cond, one.start)

    dims = []
    m = 2
    while m < R:
        dims.append(m)
        m *= 2
    seqs = (dims + [1], dims[::-1] + [1])
    even = list(range(2, R, 2))

    def move(v, d):
        for m in seqs[0]:
            if d & m:
                v = flip(v, m)
        return v

    barrier = pltpu.get_barrier_semaphore()

    @pl.loop(1, C)
    def _(d):
        pl.semaphore_signal(barrier, inc=1, device_id={"pcol": lax.rem(c + d, C)}, device_id_type=MESH)

    for d in even + [1]:
        pl.semaphore_signal(barrier, inc=1, device_id={"prow": move(r, d)}, device_id_type=MESH)
    pl.semaphore_wait(barrier, C - 1 + len(even) + 1)

    DIA = KF
    dia_plane = KS // R // A

    def z_copy(kind, source, place):
        if kind is DIA:
            src, dst, at = pan_all.at[KS // R], diag, (KF, 0)
        else:
            src = dst = ftri.at[slot(r), kind * C + source]
            at = (kind, source)
        return pltpu.make_async_remote_copy(
            src_ref=src, dst_ref=dst, send_sem=z_send.at[at[0]], recv_sem=z_recv.at[at],
            device_id={"pcol": place}, device_id_type=MESH,
        )

    def z_cond(kind, source):
        if kind is DIA:
            return jnp.logical_and(k_own, source == dia_plane)
        return kind * C + source < tiles_of(r)

    def z_start(kind):
        @pl.when(z_cond(kind, c))
        def _():
            for d in range(1, C):
                z_copy(kind, c, lax.rem(c + d, C)).start()

    def z_wait_send(kind):
        @pl.when(z_cond(kind, c))
        def _():
            some = ftri.at[0, pl.ds(0, C - 1)]
            pltpu.make_async_remote_copy(
                src_ref=some, dst_ref=some, send_sem=z_send.at[kind], recv_sem=z_recv.at[0, 0],
                device_id={"pcol": c}, device_id_type=MESH,
            ).wait_send()

    def n_copy(source, way):
        ref = pan_all.at[pl.ds(source * A, A)]
        return pltpu.make_async_remote_copy(
            src_ref=ref, dst_ref=ref, send_sem=n_send.at[way, source], recv_sem=n_recv.at[source],
            device_id={"pcol": jnp.clip(c + (1 if way else -1), 0, C - 1)}, device_id_type=MESH,
        )

    def n_pass(dist):
        for way in (1, 0):
            source = c - dist if way else c + dist
            has = source >= 0 if way else source < C
            more = c < C - 1 if way else c > 0

            @pl.when(has)
            def _(way=way, source=source, more=more):
                if dist:
                    n_copy(source, way).wait_recv()

                @pl.when(more)
                def _():
                    n_copy(source, way).start()

    def n_done():
        @pl.loop(0, C)
        def _(source):
            @pl.when(jnp.logical_and(source <= c, c < C - 1))
            def _():
                n_copy(source, 1).wait_send()

            @pl.when(jnp.logical_and(source >= c, c > 0))
            def _():
                n_copy(source, 0).wait_send()

    DG, PS, CL = SPLIT, SPLIT + 1, 2 * SPLIT + 1

    def wanted(s):
        return KS + 1 + s * C + c

    def place(kind, row):
        if kind < DG:
            return brow.at[slot(row), pl.ds(kind * H, H)]
        if kind == DG:
            return diag
        if kind < CL:
            return ps.at[pl.ds((kind - PS) * H, H)]
        return col.at[kind - CL]

    T0 = KS * SPLIT + 1 + SPLIT + CTD

    def p_index(kind, row):
        if kind < DG:
            return slot(row) * SPLIT + kind
        return KS * SPLIT + kind - DG

    def t_index(j, row):
        return T0 + lax.div(row * (row - 1), 2) + j

    def p_cond(kind, row):
        if kind < DG:
            return True if full else row < KS
        if kind < CL:
            return row == KS % R
        return row == lax.rem(wanted(kind - CL), R)

    def in_order(row, j, order):
        last = row >= 3 * R // 4
        odd_one = lax.rem(j, 2) == 1
        high = jnp.logical_and(row >= R // 2, jnp.logical_not(jnp.logical_and(last, odd_one)))
        return high if order else jnp.logical_not(high)

    def nth(q):
        k = lax.div(q, KF)
        away = jnp.where(lax.rem(k, 2) == 1, lax.div(k + 1, 2), C - lax.div(k, 2))
        return lax.rem(q, KF) * C + lax.rem(c + away, C)

    def p_copy(index, ref, d, sem=None):
        return pltpu.make_async_remote_copy(
            src_ref=ref, dst_ref=ref, send_sem=p_send.at[0] if sem is None else sem, recv_sem=p_recv.at[index],
            device_id={"prow": move(r, d)}, device_id_type=MESH,
        )

    def outs(d, order):
        if order == 2:
            return [1] if d else even + [1]
        seq = seqs[order]
        at = max([n for n, m in enumerate(seq) if d & m], default=-1)
        return seq[at + 1:]

    def pass_on(index, ref, d, order, s=None):
        if d:
            p_copy(index, ref, 1).wait_recv()
        for m in outs(d, order):
            p_copy(index, ref, m, None if s is None else c_send.at[s, m // 2]).start()

    def spread(d, kinds):
        row = move(r, d)
        for kind in kinds:
            @pl.when(p_cond(kind, row))
            def _(kind=kind):
                ref = place(kind, row)
                if kind >= DG:
                    pass_on(p_index(kind, row), ref, d, 2, kind - PS if kind > DG else None)
                else:
                    for order in range(2):
                        @pl.when(in_order(row, kind, order))
                        def _(order=order):
                            pass_on(p_index(kind, row), ref, d, order)

    def spread_tile(d, q):
        row = move(r, d)
        j = nth(q)

        @pl.when(j < tiles_of(row))
        def _():
            for order in range(2):
                @pl.when(in_order(row, j, order))
                def _(order=order):
                    pass_on(t_index(j, row), ftri.at[slot(row), j], d, order)

    def sent(k):
        total = 0
        for d in [0] + even:
            t = k ^ d

            def count(j):
                high = t >= R // 2 and not (t >= 3 * R // 4 and j % 2 == 1)
                return len(outs(d, int(high)))

            if t < KS:
                total += sum(count(n) for n in range(SPLIT)) + sum(count(j) for j in range(t))
            if t == KS % R:
                total += len(outs(d, 2))
        return total

    def drain():
        for k in range(R):
            if sent(k):
                @pl.when(r == k)
                def _(k=k):
                    whole, part = divmod(sent(k), KS)
                    for some in ([ftri.at[pl.ds(0, whole)]] if whole else []) + ([ftri.at[0, pl.ds(0, part)]] if part else []):
                        p_copy(0, some, 1).wait_send()
        for kind in psol + cols:
            for d in [0] + even:
                @pl.when(p_cond(kind, move(r, d)))
                def _(kind=kind, d=d):
                    for m in outs(d, 2):
                        p_copy(0, place(kind, KS % R), m, c_send.at[kind - PS, m // 2]).wait_send()

    def odd(row, kinds, tiles=False):
        @pl.when(lax.rem(r + row, 2) == 1)
        def _():
            for kind in kinds:
                when(p_cond(kind, row), lambda kind=kind: p_copy(p_index(kind, row), place(kind, row), 1).wait_recv())
            if tiles:
                def one(j, carry):
                    p_copy(t_index(j, row), ftri.at[slot(row), j], 1).wait_recv()
                    return carry

                lax.fori_loop(0, tiles_of(row), one, 0)

    near = [d for d in even if d & (d - 1) == 0]
    far = [d for d in even if d & (d - 1) != 0]
    bs = tuple(range(DG))
    psol = tuple(range(PS, CL))
    cols = tuple(range(CL, CL + CTD))

    loads[0].wait()
    z_start(DIA)

    @pl.when(z_cond(DIA, c))
    def _():
        diag[...] = pan_all[KS // R]
        spread(0, (DG,))

    loads[1].wait()
    loads[3].wait()
    for s in range(KF):
        @pl.when(z_cond(s, c))
        def _(s=s):
            ftri[slot(r), s * C + c] = dot(dtile[...], ftop[pl.ds(s, TILE, stride=KF), :])

        z_start(s)

    @pl.when(jnp.logical_and(k_own, c != dia_plane))
    def _():
        z_copy(DIA, 0, c).wait_recv()
        spread(0, (DG,))


    def scale_rhs():
        loads[2].wait()
        brow[mine] = dot(dtile[...], braw[...])

    when(b_own, scale_rhs)
    spread(0, bs)

    def own_tile(q, carry):
        j = nth(q)
        source = lax.rem(j, C)

        @pl.when(jnp.logical_and(j < tiles_of(r), source != c))
        def _():
            ref = ftri.at[slot(r), j]
            pltpu.make_async_remote_copy(
                src_ref=ref, dst_ref=ref, send_sem=z_send.at[0], recv_sem=z_recv.at[lax.div(j, C), source],
                device_id={"pcol": c}, device_id_type=MESH,
            ).wait_recv()

        spread_tile(0, q)
        return carry

    n_pass(0)
    lax.fori_loop(0, KS, own_tile, 0)

    x_plane = jnp.where(c >= C // 2, C // 2 - 1, C // 2)
    x_slot = jnp.where(c >= C // 2, c - C // 2, C // 2 - 1 - c)

    def x_copy(k):
        return pltpu.make_async_remote_copy(
            src_ref=fbuf.at[pl.ds(I - EARLY, EARLY)], dst_ref=xbuf.at[k], send_sem=x_send.at[0], recv_sem=x_recv.at[k],
            device_id={"pcol": x_plane}, device_id_type=MESH,
        )

    loads[4].wait()
    if EARLY:
        x_copy(x_slot).start()

    for d in even:
        spread(d, (DG,))
    odd(KS % R, (DG,))

    lanes = lax.broadcasted_iota(jnp.int32, (TILE, TILE), 1)
    rows = lax.broadcasted_iota(jnp.int32, (TILE, TILE), 0)
    tri[...] = diag[...]
    inv[...] = jnp.where(lanes == rows, 1.0, 0.0)

    lane = lanes[0:1]
    at_row = rows[:, 0:1]

    def pick(mask, values):
        return jnp.sum(jnp.where(mask, values, 0.0), axis=1, keepdims=True)

    def eliminate(b, carry):
        k = b * NB
        whole = tri[...]
        row = [tri[pl.ds(k + i, 1), :] for i in range(NB)]
        wrow = [inv[pl.ds(k + i, 1), :] for i in range(NB)]
        column = [pick(lanes == k + i, whole) for i in range(NB)]
        pivot = [[pick(lane == k + j, row[i]) if j >= i else None for j in range(NB)] for i in range(NB)]
        for i in range(NB):
            for h in range(i):
                factor_hi = pivot[h][i]
                for j in range(i, NB):
                    pivot[i][j] = pivot[i][j] - factor_hi * pivot[h][j]
                row[i] = row[i] - factor_hi * row[h]
                wrow[i] = wrow[i] - factor_hi * wrow[h]
                column[i] = column[i] - factor_hi * column[h]
            scale = 1.0 / jnp.sqrt(pivot[i][i])
            for j in range(i, NB):
                pivot[i][j] = pivot[i][j] * scale
            row[i] = jnp.where(lane >= k + i, row[i] * scale, 0.0)
            wrow[i] = wrow[i] * scale
            column[i] = column[i] * scale
        rest = inv[...]
        for i in range(NB):
            lcol = jnp.where(at_row > k + NB - 1, column[i], 0.0)
            whole = whole - lcol * row[i]
            rest = rest - lcol * wrow[i]
        tri[...] = whole
        inv[...] = rest
        for i in range(NB):
            tri[pl.ds(k + i, 1), :] = row[i]
            inv[pl.ds(k + i, 1), :] = wrow[i]
        return carry

    rounds = KS // 2 + 1
    count = 1 + 4 * rounds
    blocks = TILE // NB
    each = blocks // count
    done = count * each

    def part(n):
        lax.fori_loop(jnp.minimum(n * each, blocks), jnp.minimum((n + 1) * each, blocks), eliminate, 0)

    for d in near:
        spread(d, bs)
    part(0)
    for d in far:
        spread(d, bs)

    def relay(n, carry):
        for p in range(2):
            for d in near:
                @pl.when(n < rounds - 1)
                def _(d=d, p=p):
                    spread_tile(d, 2 * n + p)
            part(1 + 4 * n + p)
        for p in range(2):
            for d in far:
                @pl.when(n > 0)
                def _(d=d, p=p):
                    spread_tile(d, 2 * n - 2 + p)

            part(3 + 4 * n + p)
        return carry

    n_pass(1)
    lax.fori_loop(0, rounds, relay, 0)
    for dist in range(2, C - 1):
        n_pass(dist)

    def arrived(t, carry):
        odd(t, bs)

        @pl.when(t > 0)
        def _():
            odd(t, (), True)

        return carry

    lax.fori_loop(0, KS, arrived, 0)
    for t in range(KS):
        total = brow[t]
        for j in range(t):
            total = total - dot(ftri[t, j], y[j], HIGH)
        y[t] = total


    def up_copy(n, src):
        return pltpu.make_async_remote_copy(
            src_ref=src.at[n], dst_ref=rin.at[n], send_sem=r_send.at[0], recv_sem=r_recv.at[n],
            device_id={"pcol": jnp.minimum(c + 1, C - 1)}, device_id_type=MESH,
        )

    def down_copy(n, src):
        return pltpu.make_async_remote_copy(
            src_ref=src.at[n], dst_ref=lin.at[n], send_sem=l_send.at[0], recv_sem=l_recv.at[n],
            device_id={"pcol": jnp.maximum(c - 1, 0)}, device_id_type=MESH,
        )

    def columns(tiles, plane):
        parts = [dot(tiles[pl.ds(s, TILE, stride=KF), :], y[s * C + plane], HIGH) for s in range(KF)]
        return sum(parts[1:], parts[0])

    def product(i):
        total = columns(fbuf.at[i], c)
        for h in range(SPLIT):
            n = (i - i0) * SPLIT + h
            own[n] = total[h * H:(h + 1) * H]

            @pl.when(c == 0)
            def _():
                up_copy(n, own).start()

            @pl.when(c == C - 1)
            def _():
                down_copy(n, own).start()

    loads[5].wait()
    loads[6].wait()
    for i in range(i0):
        rbuf[i] = y[i * R + r]

    def strip_row(i):
        below = jnp.where(i * R + r > KS, dot(pan_all[i], inv_t[...], HIGH), 0.0)
        for s in range(CTD):
            at = pl.ds(s, TILE, stride=CTD)
            sbuf[i, at, :] = sbuf[i, at, :] - dot(below, colt[s], HIGH)
        rbuf[i] = rbuf[i] - dot(below, ps[...], HIGH)

    def total(n):
        return jnp.where(c == 0, lin[n], jnp.where(c == C - 1, rin[n], rin[n] + lin[n] - own[n]))

    def assemble(n, carry):
        i = i0 + lax.div(n, SPLIT)
        at = pl.ds(pl.multiple_of(lax.rem(n, SPLIT) * H, H), H)
        k = i * R + r
        rbuf[i, at, :] = rbuf[i, at, :] - total(n)

        @pl.when(k < KS)
        def _():
            rbuf[i, at, :] = y[slot(k), at, :]

        @pl.when(k == KS)
        def _():
            rbuf[i, at, :] = ps[at, :]

        return carry

    M = 4
    late = -(-(blocks - done) // (M + 2))
    far_lag = (C - 1) * SKEW
    P0 = far_lag + SPLIT - 1
    S0 = P0 + 5
    ROWS = 2

    def rows_done(m):
        return jnp.clip(ROWS * (m - S0 + 1), 0, I - i0)

    def chunks_done(m):
        return jnp.clip(jnp.minimum(m - far_lag + 1, SPLIT * rows_done(m)), 0, N)

    def step(m, carry):
        nr = m - c * SKEW
        nl = m - (C - 1 - c) * SKEW

        @pl.when(m < I - i0)
        def _():
            product(m + i0)

        @pl.when(jnp.logical_and(c > 0, jnp.logical_and(nr >= 0, nr < jnp.where(c == C - 2, NS, N))))
        def _():
            up_copy(nr, rin).wait_recv()
            rin[nr] = rin[nr] + own[nr]

            @pl.when(jnp.logical_and(c < C - 1, nr < NS))
            def _():
                up_copy(nr, rin).start()

        @pl.when(jnp.logical_and(c < C - 1, jnp.logical_and(nl >= 0, nl < jnp.where(c == 1, NS, N))))
        def _():
            down_copy(nl, lin).wait_recv()
            lin[nl] = lin[nl] + own[nl]

            @pl.when(jnp.logical_and(c > 0, nl < NS))
            def _():
                down_copy(nl, lin).start()

        @pl.when(m < M + 2)
        def _():
            at = done + m * late
            lax.fori_loop(jnp.minimum(at, blocks), jnp.minimum(at + late, blocks), eliminate, 0)

        @pl.when(m == M + 2)
        def _():
            inv_t[...] = inv[...].T

        @pl.when(m == M)
        def _():
            n_pass(C - 1)
            for s in range(CTD):
                @pl.when(p_cond(CL + s, r))
                def _(s=s):
                    col[s] = pan_all[lax.div(wanted(s), R)]

            spread(0, cols)

        @pl.when(m == M + 2)
        def _():
            for d in even:
                spread(d, cols)

        @pl.when(m == M + 3)
        def _():
            for a in range(A):
                tile_a = (c * A + a) * R + r
                pbuf[a] = jnp.where(tile_a > KS, dot(pan_all[c * A + a], inv_t[...]), 0.0)

                @pl.when(tile_a == KS)
                def _(a=a):
                    pbuf[a] = tri[...].T

        @pl.when(m == M + 4)
        def _():
            for s in range(CTD):
                odd(lax.rem(wanted(s), R), (CL + s,))
            for s in range(CTD):
                colt[s] = dot(col[s], inv_t[...]).T

        @pl.when(jnp.logical_and(m == P0, k_own))
        def _():
            for h in range(SPLIT):
                rest[pl.ds(h * H, H), :] = rbuf[i0, pl.ds(h * H, H), :] - total(h)
            ps[...] = dot(inv[...], rest[...])
            spread(0, psol)

        @pl.when(m == P0 + 3)
        def _():
            for d in even:
                spread(d, psol)

        @pl.when(m == P0 + 4)
        def _():
            odd(KS % R, psol)

        def one_row(n, carry):
            strip_row(n + i0)
            return carry

        lax.fori_loop(rows_done(m - 1), rows_done(m), one_row, 0)
        lax.fori_loop(chunks_done(m - 1), chunks_done(m), assemble, 0)
        return carry

    def whole_sum(e, carry):
        i = I - EARLY + e
        mine = columns(fbuf.at[i], c)
        whole = mine
        for k in range(2):
            whole = whole + columns(xbuf.at[k, e], jnp.where(c >= C // 2, C // 2 - 1 - k, C // 2 + k))
        for h in range(SPLIT):
            n = NS + e * SPLIT + h

            @pl.when(c < C // 2)
            def _():
                lin[n] = whole[h * H:(h + 1) * H]
                down_copy(n, lin).start()

            @pl.when(c >= C // 2)
            def _():
                rin[n] = whole[h * H:(h + 1) * H]
                up_copy(n, rin).start()

        return carry

    if EARLY:
        @pl.when(jnp.logical_and(c > 0, c < C - 1))
        def _():
            for k in range(2):
                x_copy(k).wait_recv()
            lax.fori_loop(0, EARLY, whole_sum, 0)

    lax.fori_loop(0, N + far_lag, step, 0)

    for kind in range(KF):
        z_wait_send(kind)
    z_wait_send(DIA)
    n_done()
    drain()

    if EARLY:
        x_copy(0).wait_send()

    def all_sent(buf, sem, count):
        some = buf.at[pl.ds(0, count)]
        pltpu.make_async_remote_copy(
            src_ref=some, dst_ref=some, send_sem=sem.at[0], recv_sem=x_recv.at[0],
            device_id={"pcol": c}, device_id_type=MESH,
        ).wait_send()

    fewer = EARLY > 0
    for bound, short, buf, sem in ((c < C - 1, C // 2 - 1, rin, r_send), (c > 0, C // 2, lin, l_send)):
        @pl.when(jnp.logical_and(bound, c != short) if fewer else bound)
        def _(buf=buf, sem=sem):
            all_sent(buf, sem, N)

        if fewer:
            @pl.when(c == short)
            def _(buf=buf, sem=sem):
                all_sent(buf, sem, NS)


def per_device(panel, strip, factor, inv_diag, rhs):
    R = lax.axis_size("prow")
    C = lax.axis_size("pcol")
    A, TILE, _ = panel.shape
    I, _, CTD, _ = strip.shape
    KF = factor.shape[2]
    NR = rhs.shape[2]
    KS = KF * C
    assert KS <= R and R & (R - 1) == 0 and KS % 2 == 0 and NR == SPLIT * TILE
    f32 = jnp.float32
    N = (I - KS // R) * SPLIT
    H = TILE // SPLIT
    early = EARLY_TILES if C == 4 else 0
    dma = pltpu.SemaphoreType.DMA
    shapes = (panel.shape, (I, TILE * CTD, TILE), rhs.shape)
    done = pl.pallas_call(
        functools.partial(kernel, R, C, CTD, KF),
        out_shape=[pltpu.VMEM(shape, f32) for shape in shapes],
        in_specs=[pl.BlockSpec(memory_space=pltpu.HBM)] * 5,
        out_specs=[pl.BlockSpec(memory_space=pltpu.VMEM)] * 3,
        scratch_shapes=[
            pltpu.VMEM((I, TILE, TILE), f32),
            pltpu.VMEM((TILE, TILE), f32),
            pltpu.VMEM((CTD, TILE, TILE), f32),
            pltpu.VMEM((CTD, TILE, TILE), f32),
            pltpu.VMEM((TILE * KF, TILE), f32),
            pltpu.VMEM((TILE, NR), f32),
            pltpu.VMEM((TILE, TILE), f32),
            pltpu.VMEM((KS, KS, TILE, TILE), f32),
            pltpu.VMEM((KS, TILE, NR), f32),
            pltpu.VMEM((KS, TILE, NR), f32),
            pltpu.VMEM((I, TILE * KF, TILE), f32),
            pltpu.VMEM((2, early, TILE * KF, TILE), f32),
            pltpu.VMEM((N, H, NR), f32),
            pltpu.VMEM((N, H, NR), f32),
            pltpu.VMEM((N, H, NR), f32),
            pltpu.VMEM((TILE, TILE), f32),
            pltpu.VMEM((TILE, TILE), f32),
            pltpu.VMEM((TILE, TILE), f32),
            pltpu.VMEM((TILE, NR), f32),
            pltpu.VMEM((TILE, NR), f32),
            dma((KF + 1,)),
            dma((KF + 1, C)),
            dma((2, C)),
            dma((C,)),
            dma((1,)),
            dma((KS * SPLIT + 1 + SPLIT + CTD + KS * (KS - 1) // 2,)),
            dma((SPLIT + CTD, R // 2)),
            dma((1,)),
            dma((2,)),
            dma((1,)),
            dma((N,)),
            dma((1,)),
            dma((N,)),
            dma((7,)),
        ],
        compiler_params=pltpu.CompilerParams(
            collective_id=0, has_side_effects=True, vmem_limit_bytes=44 << 20
        ),
    )(
        *(
            pltpu.with_memory_space_constraint(one, pltpu.HBM)
            for one in (
                panel,
                strip.reshape(I, TILE * CTD, TILE),
                factor.reshape(I, TILE * KF, TILE),
                inv_diag,
                rhs,
            )
        )
    )
    panel_factor, new_strip, forward = pl.pallas_call(
        copies,
        out_shape=[jax.ShapeDtypeStruct(shape, f32) for shape in shapes],
        in_specs=[pl.BlockSpec(memory_space=pltpu.VMEM)] * 3,
        out_specs=[pl.BlockSpec(memory_space=pl.ANY)] * 3,
        scratch_shapes=[dma((3,))],
        compiler_params=pltpu.CompilerParams(vmem_limit_bytes=16 << 20),
    )(*done)
    return panel_factor, new_strip.reshape(strip.shape), forward


def solution(mesh):
    in_specs = (
        P("pcol", "prow", None),
        P(None, "prow", None, "pcol"),
        P(None, "prow", None, "pcol"),
        P(),
        P(None, "prow", None),
    )
    out_specs = (P("pcol", "prow", None), P(None, "prow", None, "pcol"), P(None, "prow", None))
    return jax.shard_map(
        per_device, mesh=mesh, in_specs=in_specs, out_specs=out_specs, check_vma=False
    )
```

```python
import functools

import jax
import jax.numpy as jnp
from jax import lax
from jax.experimental import pallas as pl
from jax.experimental.pallas import tpu as pltpu
from jax.sharding import PartitionSpec as P

HIGHEST = lax.Precision.HIGHEST
HIGH = lax.Precision.HIGH
MESH = pl.DeviceIdType.MESH
SPLIT = 2
EARLY_TILES = 1
SKEW = 3
NB = 4


def dot(a, b, precision=HIGHEST):
    return jnp.dot(a, b, precision=precision, preferred_element_type=jnp.float32)


def when(cond, body):
    if cond is True:
        body()
    elif cond is not False:
        pl.when(cond)(body)


def flip(v, m):
    return v + m - 2 * m * lax.rem(lax.div(v, m), 2)


def copies(panel, strip, forward, panel_out, strip_out, forward_out, sem):
    pairs = ((forward, forward_out), (strip, strip_out), (panel, panel_out))
    made = [pltpu.make_async_copy(src, dst, sem.at[n]) for n, (src, dst) in enumerate(pairs)]
    for one in made:
        one.start()
    for one in made:
        one.wait()


def kernel(
    R, C, CTD, KF,
    panel, strip, factor, inv_diag, rhs,
    pbuf, sbuf, rbuf,
    pan_all, diag, col, colt, ftop, braw, dtile, ftri, brow, y, fbuf, xbuf, own, rin, lin, tri, inv, inv_t, ps, rest,
    z_send, z_recv, n_send, n_recv, p_send, p_recv, c_send, x_send, x_recv, r_send, r_recv, l_send, l_recv, in_sem,
):
    r = lax.axis_index("prow")
    c = lax.axis_index("pcol")
    A, TILE, _ = panel.shape
    I = factor.shape[0]
    KS = KF * C
    full = KS == R
    i0 = KS // R
    H = TILE // SPLIT
    N = (I - i0) * SPLIT
    EARLY = xbuf.shape[1]
    NS = N - EARLY * SPLIT

    def slot(row):
        return jnp.minimum(row, KS - 1)

    def tiles_of(row):
        return jnp.where(row < KS, row, 0)

    b_own = True if full else r < KS
    k_own = r == KS % R
    mine = jnp.minimum(r, KS - 1)

    def load(n, src, dst):
        return pltpu.make_async_copy(src, dst, in_sem.at[n])

    loads = [
        load(0, panel, pan_all.at[pl.ds(c * A, A)]),
        load(1, factor.at[0], ftop),
        load(2, rhs.at[0], braw),
        load(3, inv_diag.at[mine], dtile),
        load(4, factor, fbuf),
        load(5, rhs, rbuf),
        load(6, strip, sbuf),
    ]
    conds = [True, True, b_own, True, True, True, True]
    for cond, one in zip(conds, loads):
        when(cond, one.start)

    dims = []
    m = 2
    while m < R:
        dims.append(m)
        m *= 2
    seqs = (dims + [1], dims[::-1] + [1])
    even = list(range(2, R, 2))

    def move(v, d):
        for m in seqs[0]:
            if d & m:
                v = flip(v, m)
        return v

    barrier = pltpu.get_barrier_semaphore()

    @pl.loop(1, C)
    def _(d):
        pl.semaphore_signal(barrier, inc=1, device_id={"pcol": lax.rem(c + d, C)}, device_id_type=MESH)

    for d in even + [1]:
        pl.semaphore_signal(barrier, inc=1, device_id={"prow": move(r, d)}, device_id_type=MESH)
    pl.semaphore_wait(barrier, C - 1 + len(even) + 1)

    DIA = KF
    dia_plane = KS // R // A

    def z_copy(kind, source, place):
        if kind is DIA:
            src, dst, at = pan_all.at[KS // R], diag, (KF, 0)
        else:
            src = dst = ftri.at[slot(r), kind * C + source]
            at = (kind, source)
        return pltpu.make_async_remote_copy(
            src_ref=src, dst_ref=dst, send_sem=z_send.at[at[0]], recv_sem=z_recv.at[at],
            device_id={"pcol": place}, device_id_type=MESH,
        )

    def z_cond(kind, source):
        if kind is DIA:
            return jnp.logical_and(k_own, source == dia_plane)
        return kind * C + source < tiles_of(r)

    def z_start(kind):
        @pl.when(z_cond(kind, c))
        def _():
            for d in range(1, C):
                z_copy(kind, c, lax.rem(c + d, C)).start()

    def z_wait_send(kind):
        @pl.when(z_cond(kind, c))
        def _():
            some = ftri.at[0, pl.ds(0, C - 1)]
            pltpu.make_async_remote_copy(
                src_ref=some, dst_ref=some, send_sem=z_send.at[kind], recv_sem=z_recv.at[0, 0],
                device_id={"pcol": c}, device_id_type=MESH,
            ).wait_send()

    def n_copy(source, way):
        ref = pan_all.at[pl.ds(source * A, A)]
        return pltpu.make_async_remote_copy(
            src_ref=ref, dst_ref=ref, send_sem=n_send.at[way, source], recv_sem=n_recv.at[source],
            device_id={"pcol": jnp.clip(c + (1 if way else -1), 0, C - 1)}, device_id_type=MESH,
        )

    def n_pass(dist):
        for way in (1, 0):
            source = c - dist if way else c + dist
            has = source >= 0 if way else source < C
            more = c < C - 1 if way else c > 0

            @pl.when(has)
            def _(way=way, source=source, more=more):
                if dist:
                    n_copy(source, way).wait_recv()

                @pl.when(more)
                def _():
                    n_copy(source, way).start()

    def n_done():
        @pl.loop(0, C)
        def _(source):
            @pl.when(jnp.logical_and(source <= c, c < C - 1))
            def _():
                n_copy(source, 1).wait_send()

            @pl.when(jnp.logical_and(source >= c, c > 0))
            def _():
                n_copy(source, 0).wait_send()

    DG, PS, CL = SPLIT, SPLIT + 1, 2 * SPLIT + 1

    def wanted(s):
        return KS + 1 + s * C + c

    def place(kind, row):
        if kind < DG:
            return brow.at[slot(row), pl.ds(kind * H, H)]
        if kind == DG:
            return diag
        if kind < CL:
            return ps.at[pl.ds((kind - PS) * H, H)]
        return col.at[kind - CL]

    T0 = KS * SPLIT + 1 + SPLIT + CTD

    def p_index(kind, row):
        if kind < DG:
            return slot(row) * SPLIT + kind
        return KS * SPLIT + kind - DG

    def t_index(j, row):
        return T0 + lax.div(row * (row - 1), 2) + j

    def p_cond(kind, row):
        if kind < DG:
            return True if full else row < KS
        if kind < CL:
            return row == KS % R
        return row == lax.rem(wanted(kind - CL), R)

    def in_order(row, j, order):
        last = row >= 3 * R // 4
        odd_one = lax.rem(j, 2) == 1
        high = jnp.logical_and(row >= R // 2, jnp.logical_not(jnp.logical_and(last, odd_one)))
        return high if order else jnp.logical_not(high)

    def nth(q):
        k = lax.div(q, KF)
        away = jnp.where(lax.rem(k, 2) == 1, lax.div(k + 1, 2), C - lax.div(k, 2))
        return lax.rem(q, KF) * C + lax.rem(c + away, C)

    def p_copy(index, ref, d, sem=None):
        return pltpu.make_async_remote_copy(
            src_ref=ref, dst_ref=ref, send_sem=p_send.at[0] if sem is None else sem, recv_sem=p_recv.at[index],
            device_id={"prow": move(r, d)}, device_id_type=MESH,
        )

    def outs(d, order):
        if order == 2:
            return [1] if d else even + [1]
        seq = seqs[order]
        at = max([n for n, m in enumerate(seq) if d & m], default=-1)
        return seq[at + 1:]

    def pass_on(index, ref, d, order, s=None):
        if d:
            p_copy(index, ref, 1).wait_recv()
        for m in outs(d, order):
            p_copy(index, ref, m, None if s is None else c_send.at[s, m // 2]).start()

    def spread(d, kinds):
        row = move(r, d)
        for kind in kinds:
            @pl.when(p_cond(kind, row))
            def _(kind=kind):
                ref = place(kind, row)
                if kind >= DG:
                    pass_on(p_index(kind, row), ref, d, 2, kind - PS if kind > DG else None)
                else:
                    for order in range(2):
                        @pl.when(in_order(row, kind, order))
                        def _(order=order):
                            pass_on(p_index(kind, row), ref, d, order)

    def spread_tile(d, q):
        row = move(r, d)
        j = nth(q)

        @pl.when(j < tiles_of(row))
        def _():
            for order in range(2):
                @pl.when(in_order(row, j, order))
                def _(order=order):
                    pass_on(t_index(j, row), ftri.at[slot(row), j], d, order)

    def sent(k):
        total = 0
        for d in [0] + even:
            t = k ^ d

            def count(j):
                high = t >= R // 2 and not (t >= 3 * R // 4 and j % 2 == 1)
                return len(outs(d, int(high)))

            if t < KS:
                total += sum(count(n) for n in range(SPLIT)) + sum(count(j) for j in range(t))
            if t == KS % R:
                total += len(outs(d, 2))
        return total

    def drain():
        for k in range(R):
            if sent(k):
                @pl.when(r == k)
                def _(k=k):
                    whole, part = divmod(sent(k), KS)
                    for some in ([ftri.at[pl.ds(0, whole)]] if whole else []) + ([ftri.at[0, pl.ds(0, part)]] if part else []):
                        p_copy(0, some, 1).wait_send()
        for kind in psol + cols:
            for d in [0] + even:
                @pl.when(p_cond(kind, move(r, d)))
                def _(kind=kind, d=d):
                    for m in outs(d, 2):
                        p_copy(0, place(kind, KS % R), m, c_send.at[kind - PS, m // 2]).wait_send()

    def odd(row, kinds, tiles=False):
        @pl.when(lax.rem(r + row, 2) == 1)
        def _():
            for kind in kinds:
                when(p_cond(kind, row), lambda kind=kind: p_copy(p_index(kind, row), place(kind, row), 1).wait_recv())
            if tiles:
                def one(j, carry):
                    p_copy(t_index(j, row), ftri.at[slot(row), j], 1).wait_recv()
                    return carry

                lax.fori_loop(0, tiles_of(row), one, 0)

    near = [d for d in even if d & (d - 1) == 0]
    far = [d for d in even if d & (d - 1) != 0]
    bs = tuple(range(DG))
    psol = tuple(range(PS, CL))
    cols = tuple(range(CL, CL + CTD))

    loads[0].wait()
    z_start(DIA)

    @pl.when(z_cond(DIA, c))
    def _():
        diag[...] = pan_all[KS // R]
        spread(0, (DG,))

    loads[1].wait()
    loads[3].wait()
    for s in range(KF):
        @pl.when(z_cond(s, c))
        def _(s=s):
            ftri[slot(r), s * C + c] = dot(dtile[...], ftop[pl.ds(s, TILE, stride=KF), :])

        z_start(s)

    @pl.when(jnp.logical_and(k_own, c != dia_plane))
    def _():
        z_copy(DIA, 0, c).wait_recv()
        spread(0, (DG,))


    def scale_rhs():
        loads[2].wait()
        brow[mine] = dot(dtile[...], braw[...])

    when(b_own, scale_rhs)
    spread(0, bs)

    def own_tile(q, carry):
        j = nth(q)
        source = lax.rem(j, C)

        @pl.when(jnp.logical_and(j < tiles_of(r), source != c))
        def _():
            ref = ftri.at[slot(r), j]
            pltpu.make_async_remote_copy(
                src_ref=ref, dst_ref=ref, send_sem=z_send.at[0], recv_sem=z_recv.at[lax.div(j, C), source],
                device_id={"pcol": c}, device_id_type=MESH,
            ).wait_recv()

        spread_tile(0, q)
        return carry

    n_pass(0)
    lax.fori_loop(0, KS, own_tile, 0)

    x_plane = jnp.where(c >= C // 2, C // 2 - 1, C // 2)
    x_slot = jnp.where(c >= C // 2, c - C // 2, C // 2 - 1 - c)

    def x_copy(k):
        return pltpu.make_async_remote_copy(
            src_ref=fbuf.at[pl.ds(I - EARLY, EARLY)], dst_ref=xbuf.at[k], send_sem=x_send.at[0], recv_sem=x_recv.at[k],
            device_id={"pcol": x_plane}, device_id_type=MESH,
        )

    loads[4].wait()
    if EARLY:
        x_copy(x_slot).start()

    for d in even:
        spread(d, (DG,))
    odd(KS % R, (DG,))

    lanes = lax.broadcasted_iota(jnp.int32, (TILE, TILE), 1)
    rows = lax.broadcasted_iota(jnp.int32, (TILE, TILE), 0)
    tri[...] = diag[...]
    inv[...] = jnp.where(lanes == rows, 1.0, 0.0)

    lane = lanes[0:1]
    at_row = rows[:, 0:1]

    def pick(mask, values):
        return jnp.sum(jnp.where(mask, values, 0.0), axis=1, keepdims=True)

    def eliminate(b, carry):
        k = b * NB
        whole = tri[...]
        row = [tri[pl.ds(k + i, 1), :] for i in range(NB)]
        wrow = [inv[pl.ds(k + i, 1), :] for i in range(NB)]
        column = [pick(lanes == k + i, whole) for i in range(NB)]
        pivot = [[pick(lane == k + j, row[i]) if j >= i else None for j in range(NB)] for i in range(NB)]
        for i in range(NB):
            for h in range(i):
                factor_hi = pivot[h][i]
                for j in range(i, NB):
                    pivot[i][j] = pivot[i][j] - factor_hi * pivot[h][j]
                row[i] = row[i] - factor_hi * row[h]
                wrow[i] = wrow[i] - factor_hi * wrow[h]
                column[i] = column[i] - factor_hi * column[h]
            scale = 1.0 / jnp.sqrt(pivot[i][i])
            for j in range(i, NB):
                pivot[i][j] = pivot[i][j] * scale
            row[i] = jnp.where(lane >= k + i, row[i] * scale, 0.0)
            wrow[i] = wrow[i] * scale
            column[i] = column[i] * scale
        rest = inv[...]
        for i in range(NB):
            lcol = jnp.where(at_row > k + NB - 1, column[i], 0.0)
            whole = whole - lcol * row[i]
            rest = rest - lcol * wrow[i]
        tri[...] = whole
        inv[...] = rest
        for i in range(NB):
            tri[pl.ds(k + i, 1), :] = row[i]
            inv[pl.ds(k + i, 1), :] = wrow[i]
        return carry

    rounds = KS // 2 + 1
    blocks = TILE // NB

    for d in near:
        spread(d, bs)
    for d in far:
        spread(d, bs)

    def relay(n, carry):
        for p in range(2):
            for d in near:
                @pl.when(n < rounds - 1)
                def _(d=d, p=p):
                    spread_tile(d, 2 * n + p)
        for p in range(2):
            for d in far:
                @pl.when(n > 0)
                def _(d=d, p=p):
                    spread_tile(d, 2 * n - 2 + p)

        return carry

    n_pass(1)
    lax.fori_loop(0, rounds, relay, 0)
    for dist in range(2, C - 1):
        n_pass(dist)

    def arrived(t, carry):
        odd(t, bs)

        @pl.when(t > 0)
        def _():
            odd(t, (), True)

        return carry

    lax.fori_loop(0, KS, arrived, 0)
    for t in range(KS):
        total = brow[t]
        for j in range(t):
            total = total - dot(ftri[t, j], y[j], HIGH)
        y[t] = total


    def up_copy(n, src):
        return pltpu.make_async_remote_copy(
            src_ref=src.at[n], dst_ref=rin.at[n], send_sem=r_send.at[0], recv_sem=r_recv.at[n],
            device_id={"pcol": jnp.minimum(c + 1, C - 1)}, device_id_type=MESH,
        )

    def down_copy(n, src):
        return pltpu.make_async_remote_copy(
            src_ref=src.at[n], dst_ref=lin.at[n], send_sem=l_send.at[0], recv_sem=l_recv.at[n],
            device_id={"pcol": jnp.maximum(c - 1, 0)}, device_id_type=MESH,
        )

    def columns(tiles, plane):
        parts = [dot(tiles[pl.ds(s, TILE, stride=KF), :], y[s * C + plane], HIGH) for s in range(KF)]
        return sum(parts[1:], parts[0])

    def product(i):
        total = columns(fbuf.at[i], c)
        for h in range(SPLIT):
            n = (i - i0) * SPLIT + h
            own[n] = total[h * H:(h + 1) * H]

            @pl.when(c == 0)
            def _():
                up_copy(n, own).start()

            @pl.when(c == C - 1)
            def _():
                down_copy(n, own).start()

    loads[5].wait()
    loads[6].wait()
    for i in range(i0):
        rbuf[i] = y[i * R + r]

    def strip_row(i):
        below = jnp.where(i * R + r > KS, dot(pan_all[i], inv_t[...], HIGH), 0.0)
        for s in range(CTD):
            at = pl.ds(s, TILE, stride=CTD)
            sbuf[i, at, :] = sbuf[i, at, :] - dot(below, colt[s], HIGH)
        rbuf[i] = rbuf[i] - dot(below, ps[...], HIGH)

    def total(n):
        return jnp.where(c == 0, lin[n], jnp.where(c == C - 1, rin[n], rin[n] + lin[n] - own[n]))

    def assemble(n, carry):
        i = i0 + lax.div(n, SPLIT)
        at = pl.ds(pl.multiple_of(lax.rem(n, SPLIT) * H, H), H)
        k = i * R + r
        rbuf[i, at, :] = rbuf[i, at, :] - total(n)

        @pl.when(k < KS)
        def _():
            rbuf[i, at, :] = y[slot(k), at, :]

        @pl.when(k == KS)
        def _():
            rbuf[i, at, :] = ps[at, :]

        return carry

    M = 4
    late = -(-blocks // (M + 2))
    far_lag = (C - 1) * SKEW
    P0 = far_lag + SPLIT - 1
    S0 = P0 + 5
    ROWS = 2

    def rows_done(m):
        return jnp.clip(ROWS * (m - S0 + 1), 0, I - i0)

    def chunks_done(m):
        return jnp.clip(jnp.minimum(m - far_lag + 1, SPLIT * rows_done(m)), 0, N)

    def step(m, carry):
        nr = m - c * SKEW
        nl = m - (C - 1 - c) * SKEW

        @pl.when(m < I - i0)
        def _():
            product(m + i0)

        @pl.when(jnp.logical_and(c > 0, jnp.logical_and(nr >= 0, nr < jnp.where(c == C - 2, NS, N))))
        def _():
            up_copy(nr, rin).wait_recv()
            rin[nr] = rin[nr] + own[nr]

            @pl.when(jnp.logical_and(c < C - 1, nr < NS))
            def _():
                up_copy(nr, rin).start()

        @pl.when(jnp.logical_and(c < C - 1, jnp.logical_and(nl >= 0, nl < jnp.where(c == 1, NS, N))))
        def _():
            down_copy(nl, lin).wait_recv()
            lin[nl] = lin[nl] + own[nl]

            @pl.when(jnp.logical_and(c > 0, nl < NS))
            def _():
                down_copy(nl, lin).start()

        @pl.when(m < M + 2)
        def _():
            at = m * late
            lax.fori_loop(jnp.minimum(at, blocks), jnp.minimum(at + late, blocks), eliminate, 0)

        @pl.when(m == M + 2)
        def _():
            inv_t[...] = inv[...].T

        @pl.when(m == M)
        def _():
            n_pass(C - 1)
            for s in range(CTD):
                @pl.when(p_cond(CL + s, r))
                def _(s=s):
                    col[s] = pan_all[lax.div(wanted(s), R)]

            spread(0, cols)

        @pl.when(m == M + 2)
        def _():
            for d in even:
                spread(d, cols)

        @pl.when(m == M + 3)
        def _():
            for a in range(A):
                tile_a = (c * A + a) * R + r
                pbuf[a] = jnp.where(tile_a > KS, dot(pan_all[c * A + a], inv_t[...]), 0.0)

                @pl.when(tile_a == KS)
                def _(a=a):
                    pbuf[a] = tri[...].T

        @pl.when(m == M + 4)
        def _():
            for s in range(CTD):
                odd(lax.rem(wanted(s), R), (CL + s,))
            for s in range(CTD):
                colt[s] = dot(col[s], inv_t[...]).T

        @pl.when(jnp.logical_and(m == P0, k_own))
        def _():
            for h in range(SPLIT):
                rest[pl.ds(h * H, H), :] = rbuf[i0, pl.ds(h * H, H), :] - total(h)
            ps[...] = dot(inv[...], rest[...])
            spread(0, psol)

        @pl.when(m == P0 + 3)
        def _():
            for d in even:
                spread(d, psol)

        @pl.when(m == P0 + 4)
        def _():
            odd(KS % R, psol)

        def one_row(n, carry):
            strip_row(n + i0)
            return carry

        lax.fori_loop(rows_done(m - 1), rows_done(m), one_row, 0)
        lax.fori_loop(chunks_done(m - 1), chunks_done(m), assemble, 0)
        return carry

    def whole_sum(e, carry):
        i = I - EARLY + e
        mine = columns(fbuf.at[i], c)
        whole = mine
        for k in range(2):
            whole = whole + columns(xbuf.at[k, e], jnp.where(c >= C // 2, C // 2 - 1 - k, C // 2 + k))
        for h in range(SPLIT):
            n = NS + e * SPLIT + h

            @pl.when(c < C // 2)
            def _():
                lin[n] = whole[h * H:(h + 1) * H]
                down_copy(n, lin).start()

            @pl.when(c >= C // 2)
            def _():
                rin[n] = whole[h * H:(h + 1) * H]
                up_copy(n, rin).start()

        return carry

    if EARLY:
        @pl.when(jnp.logical_and(c > 0, c < C - 1))
        def _():
            for k in range(2):
                x_copy(k).wait_recv()
            lax.fori_loop(0, EARLY, whole_sum, 0)

    lax.fori_loop(0, N + far_lag, step, 0)

    for kind in range(KF):
        z_wait_send(kind)
    z_wait_send(DIA)
    n_done()
    drain()

    if EARLY:
        x_copy(0).wait_send()

    def all_sent(buf, sem, count):
        some = buf.at[pl.ds(0, count)]
        pltpu.make_async_remote_copy(
            src_ref=some, dst_ref=some, send_sem=sem.at[0], recv_sem=x_recv.at[0],
            device_id={"pcol": c}, device_id_type=MESH,
        ).wait_send()

    fewer = EARLY > 0
    for bound, short, buf, sem in ((c < C - 1, C // 2 - 1, rin, r_send), (c > 0, C // 2, lin, l_send)):
        @pl.when(jnp.logical_and(bound, c != short) if fewer else bound)
        def _(buf=buf, sem=sem):
            all_sent(buf, sem, N)

        if fewer:
            @pl.when(c == short)
            def _(buf=buf, sem=sem):
                all_sent(buf, sem, NS)


def per_device(panel, strip, factor, inv_diag, rhs):
    R = lax.axis_size("prow")
    C = lax.axis_size("pcol")
    A, TILE, _ = panel.shape
    I, _, CTD, _ = strip.shape
    KF = factor.shape[2]
    NR = rhs.shape[2]
    KS = KF * C
    assert KS <= R and R & (R - 1) == 0 and KS % 2 == 0 and NR == SPLIT * TILE
    f32 = jnp.float32
    N = (I - KS // R) * SPLIT
    H = TILE // SPLIT
    early = EARLY_TILES if C == 4 else 0
    dma = pltpu.SemaphoreType.DMA
    shapes = (panel.shape, (I, TILE * CTD, TILE), rhs.shape)
    done = pl.pallas_call(
        functools.partial(kernel, R, C, CTD, KF),
        out_shape=[pltpu.VMEM(shape, f32) for shape in shapes],
        in_specs=[pl.BlockSpec(memory_space=pltpu.HBM)] * 5,
        out_specs=[pl.BlockSpec(memory_space=pltpu.VMEM)] * 3,
        scratch_shapes=[
            pltpu.VMEM((I, TILE, TILE), f32),
            pltpu.VMEM((TILE, TILE), f32),
            pltpu.VMEM((CTD, TILE, TILE), f32),
            pltpu.VMEM((CTD, TILE, TILE), f32),
            pltpu.VMEM((TILE * KF, TILE), f32),
            pltpu.VMEM((TILE, NR), f32),
            pltpu.VMEM((TILE, TILE), f32),
            pltpu.VMEM((KS, KS, TILE, TILE), f32),
            pltpu.VMEM((KS, TILE, NR), f32),
            pltpu.VMEM((KS, TILE, NR), f32),
            pltpu.VMEM((I, TILE * KF, TILE), f32),
            pltpu.VMEM((2, early, TILE * KF, TILE), f32),
            pltpu.VMEM((N, H, NR), f32),
            pltpu.VMEM((N, H, NR), f32),
            pltpu.VMEM((N, H, NR), f32),
            pltpu.VMEM((TILE, TILE), f32),
            pltpu.VMEM((TILE, TILE), f32),
            pltpu.VMEM((TILE, TILE), f32),
            pltpu.VMEM((TILE, NR), f32),
            pltpu.VMEM((TILE, NR), f32),
            dma((KF + 1,)),
            dma((KF + 1, C)),
            dma((2, C)),
            dma((C,)),
            dma((1,)),
            dma((KS * SPLIT + 1 + SPLIT + CTD + KS * (KS - 1) // 2,)),
            dma((SPLIT + CTD, R // 2)),
            dma((1,)),
            dma((2,)),
            dma((1,)),
            dma((N,)),
            dma((1,)),
            dma((N,)),
            dma((7,)),
        ],
        compiler_params=pltpu.CompilerParams(
            collective_id=0, has_side_effects=True, vmem_limit_bytes=44 << 20
        ),
    )(
        *(
            pltpu.with_memory_space_constraint(one, pltpu.HBM)
            for one in (
                panel,
                strip.reshape(I, TILE * CTD, TILE),
                factor.reshape(I, TILE * KF, TILE),
                inv_diag,
                rhs,
            )
        )
    )
    panel_factor, new_strip, forward = pl.pallas_call(
        copies,
        out_shape=[jax.ShapeDtypeStruct(shape, f32) for shape in shapes],
        in_specs=[pl.BlockSpec(memory_space=pltpu.VMEM)] * 3,
        out_specs=[pl.BlockSpec(memory_space=pl.ANY)] * 3,
        scratch_shapes=[dma((3,))],
        compiler_params=pltpu.CompilerParams(vmem_limit_bytes=16 << 20),
    )(*done)
    return panel_factor, new_strip.reshape(strip.shape), forward


def solution(mesh):
    in_specs = (
        P("pcol", "prow", None),
        P(None, "prow", None, "pcol"),
        P(None, "prow", None, "pcol"),
        P(),
        P(None, "prow", None),
    )
    out_specs = (P("pcol", "prow", None), P(None, "prow", None, "pcol"), P(None, "prow", None))
    return jax.shard_map(
        per_device, mesh=mesh, in_specs=in_specs, out_specs=out_specs, check_vma=False
    )
```
